512 devices in a mesh: seq: 64 (over z_hi, y, core), head: 8 (over x, z_lo).
Axes of the slice: x: 4, y: 8, z: 8 (z_hi: 4, z_lo: 2; z = z_hi * 2 + z_lo), core: 2. Of those that a mesh axis runs over, the one named last changes fastest.
Arguments:
- tokens: bfloat16 [8192, 2880], P('seq'), may hold values from -80 to 80
- gain: float32 [2880], replicated, may hold values from 0.1 to 1.9
- w_query: bfloat16 [2880, 4096], P('seq', 'head'), may hold values from -4 to 4
- w_key: bfloat16 [2880, 512], P('seq', 'head'), may hold values from -1 to 1
- w_value: bfloat16 [2880, 512], P('seq', 'head'), may hold values from -0.109375 to 0.109375
- w_out: bfloat16 [2880, 4096], P('seq', 'head'), may hold values from -0.09375 to 0.09375
- w_gate: float32 [2880], replicated, may hold values from -0.109375 to 0.109375
- steering: bfloat16 [16, 2880], replicated, may hold values from -5 to 5
- segment_ids: int32 [8192], P('seq'), may hold values from 0 to 31, never falling along the last dimension, each value on 1 to 512 neighbouring positions
- steer_index: int32 [8192], P('seq'), may hold values from 0 to 15
- grad_out: bfloat16 [8192, 2880], P('seq'), may hold values from -6 to 6
Outputs:
- layer_out: bfloat16 [8192, 2880], P('seq', 'head')
- grad_tokens: bfloat16 [8192, 2880], P('seq', 'head')
- steer_grad: float32 [16, 2880], P(None, 'head')
The draws below stay inside these ranges and needn't reach their ends.
Inputs may be any that keep to these rules, and one draw needn't show every extreme that they name: `segment_ids`: the ids never fall along the tokens; each id names one packed document of at most 512 tokens.
All inputs are finite; a program needn't handle non-finite values.
Results may differ from the reference program's by a relative error of at most 0.011.
Values may be sent and summed in bfloat16 or wider, within the bound.
No kernel may reach another device: no remote copies, remote signals or barrier semaphores. Data moves between devices by JAX's collectives and lax.ppermute only.
A program may use at most 64 MiB of HBM per device.

```python
import math
import jax
import jax.numpy as jnp
import numpy as np
from jax import lax

D = 2880
HD = 64
QPK = 8
WIN = 128
NSTEER = 16
TOK_DEV = 128
KVH = 8
QH = 64
TOKENS = 8192
DOCS = 32
DOC_MAX = 512


def key_matrix(key):
    base = jax.random.truncated_normal(jax.random.fold_in(key, 11), -4.0, 4.0, (D, KVH * HD), jnp.float32)
    return base * D ** (-0.5)


def draw_w_key(key, part):
    return key_matrix(key).astype(jnp.bfloat16)


def draw_w_query(key, part):
    base = jax.random.truncated_normal(jax.random.fold_in(key, 12), -4.0, 4.0, (D, QH * HD), jnp.float32) * D ** (-0.5)
    return jnp.clip(base, -4.0, 4.0).astype(jnp.bfloat16)


def draw_tokens(key, part):
    row_scale = jnp.exp(jax.random.uniform(jax.random.fold_in(key, 21), (TOKENS, 1), jnp.float32, -1.15, 1.15))
    col_scale = jnp.exp(jax.random.uniform(jax.random.fold_in(key, 22), (1, D), jnp.float32, -1.15, 1.15))
    noise = jax.random.truncated_normal(jax.random.fold_in(key, 23), -4.0, 4.0, (TOKENS, D), jnp.float32)
    return (noise * row_scale * col_scale).astype(jnp.bfloat16)


def touch_ends(drawn, rng, smallest, high):
    place = [jax.random.randint(jax.random.fold_in(rng, axis), (), 0, length) for axis, length in enumerate(drawn.shape)]
    widest = drawn.shape.index(max(drawn.shape))
    neighbour = place[:widest] + [(place[widest] + 1) % drawn.shape[widest]] + place[widest + 1:]
    return drawn.at[tuple(place)].set(smallest).at[tuple(neighbour)].set(high)


def block_scale(rng, extent, shards, low, top_value):
    loudness = 1.0
    for axis_at, blocks in shards:
        draws = jax.random.uniform(jax.random.fold_in(jax.random.fold_in(rng, 6), axis_at), (blocks,), jnp.float32, low / len(shards), top_value / len(shards))
        loudness = loudness * jnp.repeat(jnp.exp(draws), extent[axis_at] // blocks).reshape((-1,) + (1,) * (len(extent) - 1 - axis_at))
    return loudness


def length_profile(amount, total, reach, skew):
    loads = [(1 << 20) // math.isqrt(standing ** skew) + 1 for standing in range(2, amount + 1)]
    spare, holding = total - reach - (amount - 1), [1] * (amount - 1)
    while spare > 0:
        movable = [i for i in range(amount - 1) if holding[i] < reach]
        whole, budget = sum([loads[i] for i in movable]), spare
        for i in movable:
            addition = min(reach - holding[i], max(1, budget * loads[i] // whole), spare)
            holding[i] = holding[i] + addition
            spare = spare - addition
    return np.array([reach] + holding)


def ragged(key, count, total, most, slope):
    if count == 2:
        one = jax.random.randint(key, (), max(1, total - most), min(most, total - 1) + 1)
        return jnp.stack([one, total - one])
    tallies = jnp.asarray(length_profile(count, total, most, slope), jnp.int32)
    couples = (count - 1) // 2
    source_of, taker = tallies[1:1 + 2 * couples:2], tallies[2:2 + 2 * couples:2]
    margin = jnp.minimum(source_of - 1, most - taker)
    passed = jax.random.randint(jax.random.fold_in(key, 1), (couples,), 0, 1 << 20) % (margin + 1)
    tallies = tallies.at[1:1 + 2 * couples:2].set(source_of - passed).at[2:2 + 2 * couples:2].set(taker + passed)
    return tallies[jax.random.permutation(jax.random.fold_in(key, 2), count)]


def scatter_about(rng, extent, spread, most, split=(), held_as=jnp.bfloat16):
    values = jax.random.normal(rng, extent, jnp.float32) * spread
    if len(split) > 0:
        values = block_scale(rng, extent, split, -0.22, 0.18) * values
    return jnp.clip(values, min=-most, max=most).astype(held_as)


def setup_inputs(seed: int = 0) -> dict:
    splits = jax.random.split(jax.random.key(seed), 12)
    tokens = draw_tokens(jax.random.fold_in(splits[11], 71), 0)
    gain = jnp.clip(1.0 + 0.18 * jax.random.normal(splits[1], (D,), jnp.float32), 0.1, 1.9)
    w_query = draw_w_query(jax.random.fold_in(splits[11], 71), 0)
    w_key = draw_w_key(jax.random.fold_in(splits[11], 71), 0)
    w_value = scatter_about(splits[4], (D, KVH * HD), D ** -0.5, 0.109375, ((0, 64), (1, 8)))
    w_out = scatter_about(splits[5], (D, QH * HD), (QH * HD) ** -0.5, 0.09375, ((0, 64), (1, 8)))
    w_gate = scatter_about(splits[6], (D,), D ** -0.5, 0.109375, (), jnp.float32)
    steering = scatter_about(splits[7], (NSTEER, D), 1.0, 5.0)
    segment_ids = jnp.searchsorted(jnp.cumsum(ragged(splits[8], DOCS, TOKENS, DOC_MAX, 2)), jnp.arange(TOKENS), side="right").astype(jnp.int32)
    steer_index = touch_ends(jax.random.randint(splits[9], (TOKENS,), 0, NSTEER), jax.random.fold_in(splits[9], 1), 0, NSTEER - 1).astype(jnp.int32)
    grad_out = scatter_about(splits[10], (TOKENS, D), 1.0, 6.0, ((0, 64),))
    return dict(tokens=tokens, gain=gain, w_query=w_query, w_key=w_key, w_value=w_value, w_out=w_out, w_gate=w_gate, steering=steering, segment_ids=segment_ids, steer_index=steer_index, grad_out=grad_out)


EPSILON = 1e-05
HIGHEST = lax.Precision.HIGHEST

def normalize(tokens, gain):
    tokens_f = tokens.astype(jnp.float32)
    inverse = lax.rsqrt(lax.optimization_barrier(jnp.mean(tokens_f * tokens_f, axis=-1, keepdims=True)) + EPSILON)
    unit_rows = tokens_f * inverse
    return (unit_rows, inverse, (unit_rows * gain).astype(jnp.bfloat16))

def rounded(values_f):
    return lax.optimization_barrier(values_f.astype(jnp.bfloat16)).astype(jnp.float32)

def contract(left, right):
    return lax.dot_general(left, right, (((1,), (1,)), ((), ())), preferred_element_type=jnp.float32)

def band_mask(query_seg, key_seg, offset):
    query_count = query_seg.shape[0]
    key_count = key_seg.shape[0]
    query_pos = lax.broadcasted_iota(jnp.int32, (query_count, key_count), 0)
    key_pos = lax.broadcasted_iota(jnp.int32, (query_count, key_count), 1) - offset
    distance = query_pos - key_pos
    return (distance >= 0) & (distance < WIN) & (query_seg[:, None] == key_seg[None, :])

def block_probs(query_block, key_block, mask):
    scores = jnp.einsum('rgqd,kgd->gqrk', query_block.astype(jnp.float32), key_block.astype(jnp.float32)) * HD ** (-0.5)
    scores = jnp.where(mask[None, None], scores, -jnp.inf)
    highest = lax.optimization_barrier(jnp.max(scores, axis=-1, keepdims=True))
    raised = jnp.exp(scores - highest)
    return raised / lax.optimization_barrier(jnp.sum(raised, axis=-1, keepdims=True))

def reference(tokens, gain, w_query, w_key, w_value, w_out, w_gate, steering, segment_ids, steer_index, grad_out):
    unit_rows, inverse, normed = normalize(tokens, gain)
    query_all = jnp.dot(normed, w_query, preferred_element_type=jnp.float32).astype(jnp.bfloat16)
    key_all = jnp.dot(normed, w_key, preferred_element_type=jnp.float32).astype(jnp.bfloat16)
    value_all = jnp.dot(normed, w_value, preferred_element_type=jnp.float32).astype(jnp.bfloat16)
    padded_keys = jnp.concatenate([jnp.zeros((WIN, KVH * HD), jnp.bfloat16), key_all], axis=0)
    padded_values = jnp.concatenate([jnp.zeros((WIN, KVH * HD), jnp.bfloat16), value_all], axis=0)
    segment_all = segment_ids.astype(jnp.int32)
    padded_seg = jnp.concatenate([jnp.full((WIN,), -1, jnp.int32), segment_all], axis=0)
    block_ids = jnp.arange(TOKENS // TOK_DEV, dtype=jnp.int32)

    def pieces(block_id):
        start = block_id * TOK_DEV
        query_block = lax.dynamic_slice_in_dim(query_all, start, TOK_DEV, 0).reshape(TOK_DEV, KVH, QPK, HD)
        key_block = lax.dynamic_slice_in_dim(padded_keys, start, WIN + TOK_DEV, 0).reshape(WIN + TOK_DEV, KVH, HD)
        value_block = lax.dynamic_slice_in_dim(padded_values, start, WIN + TOK_DEV, 0).reshape(WIN + TOK_DEV, KVH, HD)
        query_seg = lax.dynamic_slice_in_dim(segment_all, start, TOK_DEV, 0)
        key_seg = lax.dynamic_slice_in_dim(padded_seg, start, WIN + TOK_DEV, 0)
        probs = block_probs(query_block, key_block, band_mask(query_seg, key_seg, WIN))
        return (query_block, key_block, value_block, probs)

    def forward_block(block_id):
        query_block, key_block, value_block, probs = pieces(block_id)
        mixed = jnp.einsum('gqrk,kgd->rgqd', rounded(probs), value_block.astype(jnp.float32))
        return mixed.reshape(TOK_DEV, QH * HD).astype(jnp.bfloat16)
    mixed_all = lax.map(forward_block, block_ids).reshape(TOKENS, QH * HD)
    group_cols = QPK * HD
    attn_sum = jnp.zeros((TOKENS, D), jnp.float32)
    for group_index in range(KVH):
        col_start = group_index * group_cols
        attn_sum = attn_sum + rounded(contract(mixed_all[:, col_start:col_start + group_cols], w_out[:, col_start:col_start + group_cols]))
    tokens_f = tokens.astype(jnp.float32)
    gate_value = jax.nn.sigmoid(jnp.dot(normed.astype(jnp.float32), w_gate, precision=HIGHEST))
    one_hot = (steer_index[:, None] == jnp.arange(NSTEER, dtype=jnp.int32)[None, :]).astype(jnp.float32)
    steer_rows = jnp.dot(one_hot, steering.astype(jnp.float32), precision=HIGHEST)
    layer_out = (tokens_f + attn_sum + gate_value[:, None] * steer_rows).astype(jnp.bfloat16)
    grad_f = grad_out.astype(jnp.float32)
    steer_grad = jnp.dot(one_hot.T, gate_value[:, None] * grad_f, precision=HIGHEST)
    grad_logit = gate_value * (1.0 - gate_value) * lax.optimization_barrier(jnp.sum(grad_f * steer_rows, axis=-1))
    grad_mixed = jnp.dot(grad_out, w_out, preferred_element_type=jnp.float32).astype(jnp.bfloat16)

    def backward_block(block_id):
        query_block, key_block, value_block, probs = pieces(block_id)
        start = block_id * TOK_DEV
        grad_block = lax.dynamic_slice_in_dim(grad_mixed, start, TOK_DEV, 0).reshape(TOK_DEV, KVH, QPK, HD).astype(jnp.float32)
        grad_values = jnp.einsum('gqrk,rgqd->kgd', rounded(probs), grad_block)
        grad_prob = jnp.einsum('rgqd,kgd->gqrk', grad_block, value_block.astype(jnp.float32))
        delta = lax.optimization_barrier(jnp.sum(probs * grad_prob, axis=-1, keepdims=True))
        grad_scores = rounded(probs * (grad_prob - delta) * HD ** (-0.5))
        grad_query = jnp.einsum('gqrk,kgd->rgqd', grad_scores, key_block.astype(jnp.float32)).astype(jnp.bfloat16)
        grad_keys = jnp.einsum('gqrk,rgqd->kgd', grad_scores, query_block.astype(jnp.float32))
        return (grad_query.reshape(TOK_DEV, QH * HD), grad_keys.reshape(WIN + TOK_DEV, KVH * HD), grad_values.reshape(WIN + TOK_DEV, KVH * HD))
    query_parts, key_parts, value_parts = lax.map(backward_block, block_ids)
    grad_query_all = query_parts.reshape(TOKENS, QH * HD)

    def settle(parts):
        own_rows = parts[:, WIN:]
        own_rows = own_rows.at[:-1, TOK_DEV - WIN:].add(parts[1:, :WIN])
        return own_rows.reshape(TOKENS, KVH * HD).astype(jnp.bfloat16)
    grad_key_all = settle(key_parts)
    grad_value_all = settle(value_parts)
    grad_normed = jnp.zeros((TOKENS, D), jnp.float32)
    for group_index in range(KVH):
        col_start = group_index * group_cols
        key_start = group_index * HD
        group_terms = contract(grad_query_all[:, col_start:col_start + group_cols], w_query[:, col_start:col_start + group_cols])
        group_terms = group_terms + contract(grad_key_all[:, key_start:key_start + HD], w_key[:, key_start:key_start + HD])
        group_terms = group_terms + contract(grad_value_all[:, key_start:key_start + HD], w_value[:, key_start:key_start + HD])
        grad_normed = grad_normed + rounded(group_terms)
    grad_normed = grad_normed + grad_logit[:, None] * w_gate[None, :]
    scaled = grad_normed * gain
    row_mean = lax.optimization_barrier(jnp.sum(scaled * unit_rows, axis=-1, keepdims=True)) / D
    grad_tokens = (grad_f + inverse * (scaled - unit_rows * row_mean)).astype(jnp.bfloat16)
    return (layer_out, grad_tokens, steer_grad)
```

```python
import jax
import jax.numpy as jnp
from jax import lax
from jax.sharding import Mesh, PartitionSpec as P

HD = 64
WIN = 128
EPSILON = 1e-05
HIGHEST = lax.Precision.HIGHEST
SEQ = ("zh", "y", "core")
HEAD = ("x", "zl")
F32 = jnp.float32
BF16 = jnp.bfloat16
PAD = 48


def shifted(value, by):
    count = lax.axis_size(SEQ)
    pairs = [(i, i + by) for i in range(count) if 0 <= i + by < count]
    return lax.ppermute(value, SEQ, pairs)


def gathered(value, axes):
    count = lax.axis_size(axes)
    spread = jnp.broadcast_to(value[None], (count,) + value.shape)
    return lax.all_to_all(spread, axes, 0, 0)


def dot(left, right, dims, **kw):
    return lax.dot_general(left, right, (dims, ((), ())), preferred_element_type=F32, **kw)


def blocked(rows):
    width = rows.shape[-1]
    parts = rows.reshape(4, 8, 2, -1, width).transpose(1, 0, 2, 3, 4)
    parts = jnp.pad(parts, ((0, 0), (0, 0), (0, 0), (0, PAD - parts.shape[3]), (0, 0)))
    return parts.reshape(-1, width)


def for_heads(rows):
    width = rows.shape[-1]
    parts = rows.reshape(2, 4, 4, 2, PAD, width).transpose(2, 0, 1, 3, 4, 5)
    return parts.reshape(8, -1, width)


def unpadded(rows, row_count):
    width = rows.shape[-1]
    return rows.reshape(8, PAD, width)[:, : row_count // 8].reshape(row_count, width)


def split3(value):
    high = lax.reduce_precision(value, 8, 7)
    rest = value - high
    mid = lax.reduce_precision(rest, 8, 7)
    low = lax.reduce_precision(rest - mid, 8, 7)
    return jnp.stack([high, mid, low])


def shards(
    tokens,
    gain,
    w_query,
    w_key,
    w_value,
    w_out,
    w_gate,
    steering,
    segment_ids,
    steer_index,
    grad_out,
):
    row_count, model_width = tokens.shape
    share = model_width // 8
    start = lax.axis_index(HEAD) * share

    padded = lambda w: jnp.pad(w, ((0, PAD - w.shape[0]), (0, 0)))
    both = jnp.stack([padded(w_query), padded(w_out)])
    half = both.shape[2] // 2
    both = both.reshape(2, PAD, 2, half).transpose(2, 0, 1, 3)
    sent = jnp.broadcast_to(both[None], (4,) + both.shape).reshape((8,) + both.shape[1:])
    near = lax.all_to_all(sent, ("zh", "core"), 0, 0)
    q_own = lax.all_gather(near[:, 0], "y", axis=0, tiled=True).reshape(-1, half)
    o_own = lax.all_gather(near[:, 1], "y", axis=0, tiled=True).reshape(-1, half)
    w_kv = padded(jnp.concatenate([w_key, w_value], axis=1))
    kv_near = lax.all_gather(w_kv, ("zh",), axis=0, tiled=False)
    kv_all = lax.all_gather(kv_near, ("y", "core"), axis=0, tiled=False)
    kv_all = kv_all.reshape(8, 2, 4, PAD, 2 * HD).transpose(0, 2, 1, 3, 4).reshape(-1, 2 * HD)
    flip = [(0, 1), (1, 0)]
    q_oth = lax.ppermute(q_own, "core", flip)
    o_oth = lax.ppermute(o_own, "core", flip)

    tok = tokens.T.astype(F32)
    inverse = lax.rsqrt(jnp.mean(tok * tok, axis=0, keepdims=True) + EPSILON)
    unit = tok * inverse
    normed = (unit * gain[:, None]).astype(BF16)
    normed_b = blocked(normed)
    unit_b = blocked(unit * gain[:, None])
    grad_t = grad_out.T
    grad_b = blocked(grad_t)
    gate = jax.nn.sigmoid(jnp.sum(normed.astype(F32) * w_gate[:, None], axis=0))
    one_hot = steer_index[None, :] == lax.broadcasted_iota(jnp.int32, (16, row_count), 0)
    products = dot(steering, grad_t, ((1,), (0,)))
    grad_logit = gate * (1.0 - gate) * jnp.sum(jnp.where(one_hot, products, 0.0), axis=0)
    steer_share = lax.dynamic_slice_in_dim(steering, start, share, 1)
    steer_rows = dot(steer_share, one_hot.astype(BF16), ((0,), (0,)))
    grad_share = lax.dynamic_slice_in_dim(grad_t, start, share, 0).astype(F32)
    steer_part = dot(
        one_hot.astype(F32), gate[None, :] * grad_share, ((1,), (1,)), precision=HIGHEST
    )
    steer_near = jnp.sum(gathered(steer_part, ("zh", "core")), axis=0)
    steer_grad = jnp.sum(gathered(steer_near, ("y",)), axis=0)

    halo_seg = shifted(segment_ids, 1)
    halo_seg = jnp.where(lax.axis_index(SEQ) > 0, halo_seg, -1)
    kv = dot(kv_all, normed_b, ((0,), (0,))).astype(BF16)
    kv_halo = shifted(kv, 1)
    wide = jnp.concatenate([kv_halo, kv], axis=1)
    keys, values = wide[:HD], wide[HD:]
    wide_seg = jnp.concatenate([halo_seg, segment_ids])
    query_pos = lax.broadcasted_iota(jnp.int32, (row_count, 2 * row_count), 0)
    key_pos = lax.broadcasted_iota(jnp.int32, (row_count, 2 * row_count), 1) - WIN
    distance = query_pos - key_pos
    mask = (distance >= 0) & (distance < WIN) & (segment_ids[:, None] == wide_seg[None, :])
    query = jnp.concatenate(
        [
            dot(q_own, normed_b, ((0,), (0,))).astype(BF16),
            dot(q_oth, normed_b, ((0,), (0,))).astype(BF16),
        ]
    ).reshape(8, HD, row_count)
    scores = jnp.einsum("hdq,dk->hqk", query, keys, preferred_element_type=F32) * HD**-0.5
    scores = jnp.where(mask[None], scores, -jnp.inf)
    raised = jnp.exp(scores - jnp.max(scores, axis=-1, keepdims=True))
    probs = raised / jnp.sum(raised, axis=-1, keepdims=True)
    probs_b = probs.astype(BF16)
    mixed = jnp.einsum("hqk,dk->hdq", probs_b, values, preferred_element_type=F32)
    mixed = mixed.astype(BF16).reshape(2, half, row_count)
    term = dot(o_own, mixed[0], ((1,), (0,))) + dot(o_oth, mixed[1], ((1,), (0,)))
    attn = lax.all_to_all(for_heads(term.astype(BF16)), HEAD, 0, 0)
    attn_share = unpadded(jnp.sum(attn.astype(F32), axis=0), share)
    token_share = lax.dynamic_slice_in_dim(tokens.T, start, share, 0).astype(F32)
    layer_out = (token_share + attn_share + gate[None, :] * steer_rows).astype(BF16)

    grad_mixed = jnp.concatenate(
        [
            dot(o_own, grad_b, ((0,), (0,))).astype(BF16),
            dot(o_oth, grad_b, ((0,), (0,))).astype(BF16),
        ]
    ).reshape(8, HD, row_count)
    grad_values = jnp.einsum("hqk,hdq->dk", probs_b, grad_mixed, preferred_element_type=F32)
    grad_prob = jnp.einsum("hdq,dk->hqk", grad_mixed, values, preferred_element_type=F32)
    delta = jnp.sum(probs * grad_prob, axis=-1, keepdims=True)
    grad_scores = (probs * (grad_prob - delta) * HD**-0.5).astype(BF16)
    grad_query = jnp.einsum("hqk,dk->hdq", grad_scores, keys, preferred_element_type=F32)
    grad_query = grad_query.astype(BF16).reshape(2, half, row_count)
    grad_keys = jnp.einsum("hqk,hdq->dk", grad_scores, query, preferred_element_type=F32)
    grad_kv = jnp.concatenate([grad_keys, grad_values])
    returned = shifted(grad_kv[:, :WIN].astype(BF16), -1)
    grad_kv = (grad_kv[:, WIN:] + returned.astype(F32)).astype(BF16)
    terms = (
        dot(q_own, grad_query[0], ((1,), (0,)))
        + dot(q_oth, grad_query[1], ((1,), (0,)))
        + dot(kv_all, grad_kv, ((1,), (0,)))
    ).astype(BF16)
    row_part = split3(jnp.sum(terms.astype(F32) * unit_b, axis=0)).astype(BF16)
    extra = jnp.broadcast_to(jnp.pad(row_part, ((0, 13), (0, 0)))[None], (8, 16, row_count))
    back = lax.all_to_all(jnp.concatenate([for_heads(terms), extra], axis=1), HEAD, 0, 0)
    back = jnp.sum(back.astype(F32), axis=0)
    gain_share = lax.dynamic_slice_in_dim(gain, start, share, 0)[:, None]
    gate_share = lax.dynamic_slice_in_dim(w_gate, start, share, 0)[:, None]
    total = unpadded(back[: 8 * PAD], share) + grad_logit[None, :] * gate_share
    gate_total = jnp.sum(unit * (gain * w_gate)[:, None], axis=0)
    row_total = jnp.sum(back[8 * PAD : 8 * PAD + 3], axis=0) + grad_logit * gate_total
    unit_share = token_share * inverse
    scaled = total * gain_share
    grad_tokens = (
        grad_share + inverse * (scaled - unit_share * (row_total / model_width)[None, :])
    ).astype(BF16)
    return (layer_out.T, grad_tokens.T, steer_grad)


def solution(mesh):
    split = Mesh(mesh.devices.reshape(4, 8, 2, 4, 2), SEQ + HEAD)
    placed = (
        P(SEQ, None),
        P(),
        P(SEQ, HEAD),
        P(SEQ, HEAD),
        P(SEQ, HEAD),
        P(SEQ, HEAD),
        P(),
        P(),
        P(SEQ),
        P(SEQ),
        P(SEQ, None),
    )
    return jax.shard_map(
        shards,
        mesh=split,
        in_specs=placed,
        out_specs=(P(SEQ, HEAD), P(SEQ, HEAD), P(None, HEAD)),
        check_vma=False,
    )
```

```python
import jax
import jax.numpy as jnp
from jax import lax
from jax.experimental import pallas as pl
from jax.experimental.pallas import tpu as pltpu
from jax.sharding import Mesh, PartitionSpec as P

HD = 64
WIN = 128
EPSILON = 1e-05
HIGHEST = lax.Precision.HIGHEST
SEQ = ("zh", "y", "core")
HEAD = ("x", "zl")
F32 = jnp.float32
BF16 = jnp.bfloat16
PAD = 48


def shifted(value, by):
    count = lax.axis_size(SEQ)
    pairs = [(i, i + by) for i in range(count) if 0 <= i + by < count]
    return lax.ppermute(value, SEQ, pairs)


def gathered(value, axes):
    count = lax.axis_size(axes)
    spread = jnp.broadcast_to(value[None], (count,) + value.shape)
    return lax.all_to_all(spread, axes, 0, 0)


def dot(left, right, dims, **kw):
    return lax.dot_general(left, right, (dims, ((), ())), preferred_element_type=F32, **kw)


def blocked(rows):
    width = rows.shape[-1]
    parts = rows.reshape(4, 8, 2, -1, width).transpose(1, 0, 2, 3, 4)
    parts = jnp.pad(parts, ((0, 0), (0, 0), (0, 0), (0, PAD - parts.shape[3]), (0, 0)))
    return parts.reshape(-1, width)


def for_heads(rows):
    width = rows.shape[-1]
    parts = rows.reshape(2, 4, 4, 2, PAD, width).transpose(2, 0, 1, 3, 4, 5)
    return parts.reshape(8, -1, width)


def unpadded(rows, row_count):
    width = rows.shape[-1]
    return rows.reshape(8, PAD, width)[:, : row_count // 8].reshape(row_count, width)


def split3(value):
    high = lax.reduce_precision(value, 8, 7)
    rest = value - high
    mid = lax.reduce_precision(rest, 8, 7)
    low = lax.reduce_precision(rest - mid, 8, 7)
    return jnp.stack([high, mid, low])


def mm(left, right, left_dim, right_dim):
    dims = (((left_dim,), (right_dim,)), ((), ()))
    return lax.dot_general(left, right, dims, preferred_element_type=F32)


def attend_kernel(q_own, q_oth, kv, halo, mask, mixed, probs):
    keys = jnp.concatenate([halo[:HD, :], kv[:HD, :]], axis=1)
    values = jnp.concatenate([halo[HD:, :], kv[HD:, :]], axis=1)
    allowed = mask[...] > 0.0
    for head in range(8):
        source = q_own if head < 4 else q_oth
        query = source[pl.ds(head % 4 * HD, HD), :]
        scores = mm(keys, query, 0, 0) * HD**-0.5
        scores = jnp.where(allowed, scores, -jnp.inf)
        raised = jnp.exp(scores - jnp.max(scores, axis=0, keepdims=True))
        prob = raised / jnp.sum(raised, axis=0, keepdims=True)
        probs[head] = prob
        mixed[pl.ds(head * HD, HD), :] = mm(values, prob.astype(BF16), 1, 0).astype(BF16)


def attend_back_kernel(
    g_own, g_oth, q_own, q_oth, kv, halo, probs, grad_query, grad_halo, grad_kv
):
    keys = jnp.concatenate([halo[:HD, :], kv[:HD, :]], axis=1)
    values = jnp.concatenate([halo[HD:, :], kv[HD:, :]], axis=1)
    grad_keys = jnp.zeros(keys.shape, F32)
    grad_values = jnp.zeros(keys.shape, F32)
    for head in range(8):
        rows = pl.ds(head % 4 * HD, HD)
        query = (q_own if head < 4 else q_oth)[rows, :]
        grad = (g_own if head < 4 else g_oth)[rows, :]
        prob = probs[head]
        grad_values += mm(grad, prob.astype(BF16), 1, 1)
        grad_prob = mm(values, grad, 0, 0)
        delta = jnp.sum(prob * grad_prob, axis=0, keepdims=True)
        grad_scores = (prob * (grad_prob - delta) * HD**-0.5).astype(BF16)
        grad_query[pl.ds(head * HD, HD), :] = mm(keys, grad_scores, 1, 0).astype(BF16)
        grad_keys += mm(query, grad_scores, 1, 1)
    grad_halo[:HD, :] = grad_keys[:, :WIN].astype(BF16)
    grad_halo[HD:, :] = grad_values[:, :WIN].astype(BF16)
    grad_kv[:HD, :] = grad_keys[:, WIN:]
    grad_kv[HD:, :] = grad_values[:, WIN:]


def call(kernel, outs, *args):
    size = sum(a.size * a.dtype.itemsize for a in (*args, *outs))
    return pl.pallas_call(
        kernel,
        out_shape=outs,
        compiler_params=pltpu.CompilerParams(vmem_limit_bytes=40 * 2**20),
        cost_estimate=pl.CostEstimate(flops=10**8, bytes_accessed=size, transcendentals=0),
    )(*args)


def shards(
    tokens,
    gain,
    w_query,
    w_key,
    w_value,
    w_out,
    w_gate,
    steering,
    segment_ids,
    steer_index,
    grad_out,
):
    row_count, model_width = tokens.shape
    share = model_width // 8
    start = lax.axis_index(HEAD) * share

    padded = lambda w: jnp.pad(w, ((0, PAD - w.shape[0]), (0, 0)))
    half = w_query.shape[1] // 2
    query_w, out_w = padded(w_query), padded(w_out)
    pair = lambda c: jnp.concatenate(
        [query_w[:, c * half : (c + 1) * half], out_w[:, c * half : (c + 1) * half]], axis=1
    )
    sent = jnp.stack([pair(0), pair(1)] * 4)
    near = lax.all_to_all(sent, ("zh", "core"), 0, 0)
    own = lax.all_gather(near, "y", axis=0, tiled=True).reshape(-1, 2 * half)
    w_kv = padded(jnp.concatenate([w_key, w_value], axis=1))
    w_kv, near = lax.optimization_barrier((w_kv, near))
    kv_near = lax.all_gather(w_kv, ("zh",), axis=0, tiled=False)
    kv_all = lax.all_gather(kv_near, ("y", "core"), axis=0, tiled=False)
    kv_all = kv_all.reshape(8, 2, 4, PAD, 2 * HD).transpose(0, 2, 1, 3, 4).reshape(-1, 2 * HD)

    tok = tokens.T.astype(F32)
    inverse = lax.rsqrt(jnp.mean(tok * tok, axis=0, keepdims=True) + EPSILON)
    unit = tok * inverse
    normed = (unit * gain[:, None]).astype(BF16)
    normed_b = blocked(normed)
    unit_b = blocked(unit * gain[:, None])
    grad_t = grad_out.T
    grad_b = blocked(grad_t)
    gate = jax.nn.sigmoid(jnp.sum(normed.astype(F32) * w_gate[:, None], axis=0))
    one_hot = steer_index[None, :] == lax.broadcasted_iota(jnp.int32, (16, row_count), 0)
    products = dot(steering, grad_t, ((1,), (0,)))
    grad_logit = gate * (1.0 - gate) * jnp.sum(jnp.where(one_hot, products, 0.0), axis=0)
    steer_share = lax.dynamic_slice_in_dim(steering, start, share, 1)
    steer_rows = dot(steer_share, one_hot.astype(BF16), ((0,), (0,)))
    grad_share = lax.dynamic_slice_in_dim(grad_t, start, share, 0).astype(F32)
    steer_part = dot(
        one_hot.astype(F32), gate[None, :] * grad_share, ((1,), (1,)), precision=HIGHEST
    )
    steer_near = jnp.sum(gathered(steer_part, ("zh", "core")), axis=0)
    steer_grad = jnp.sum(gathered(steer_near, ("y",)), axis=0)

    halo_seg = shifted(segment_ids, 1)
    halo_seg = jnp.where(lax.axis_index(SEQ) > 0, halo_seg, -1)
    kv = dot(kv_all, normed_b, ((0,), (0,))).astype(BF16)
    halo = shifted(kv, 1)
    wide_seg = jnp.concatenate([halo_seg, segment_ids])
    key_pos = lax.broadcasted_iota(jnp.int32, (2 * row_count, row_count), 0) - WIN
    query_pos = lax.broadcasted_iota(jnp.int32, (2 * row_count, row_count), 1)
    distance = query_pos - key_pos
    mask = (distance >= 0) & (distance < WIN) & (wide_seg[:, None] == segment_ids[None, :])
    mask = mask.astype(F32)
    own, halo, mask, steer_grad, normed_b, grad_b, unit_b, kv, kv_all = lax.optimization_barrier(
        (own, halo, mask, steer_grad, normed_b, grad_b, unit_b, kv, kv_all)
    )
    oth = lax.ppermute(own, "core", [(0, 1), (1, 0)])
    like = jax.ShapeDtypeStruct
    q_own = dot(own[:, :half], normed_b, ((0,), (0,))).astype(BF16)
    q_oth = dot(oth[:, :half], normed_b, ((0,), (0,))).astype(BF16)
    mixed, probs = call(
        attend_kernel,
        (like((2 * half, row_count), BF16), like((8, 2 * row_count, row_count), F32)),
        *(q_own, q_oth, kv, halo, mask),
    )
    term = dot(own[:, half:], mixed[:half], ((1,), (0,)))
    term = term + dot(oth[:, half:], mixed[half:], ((1,), (0,)))
    blocks = for_heads(term.astype(BF16))
    g_own = dot(own[:, half:], grad_b, ((0,), (0,))).astype(BF16)
    blocks, grad_b, own, oth = lax.optimization_barrier((blocks, grad_b, own, oth))
    attn = lax.all_to_all(blocks, HEAD, 0, 0)

    g_oth = dot(oth[:, half:], grad_b, ((0,), (0,))).astype(BF16)
    grad_query, grad_halo, grad_kv = call(
        attend_back_kernel,
        (
            like((2 * half, row_count), BF16),
            like((2 * HD, row_count), BF16),
            like((2 * HD, row_count), F32),
        ),
        *(g_own, g_oth, q_own, q_oth, kv, halo, probs),
    )
    returned = shifted(grad_halo, -1)
    grad_kv = (grad_kv + returned.astype(F32)).astype(BF16)
    terms = (
        dot(own[:, :half], grad_query[:half], ((1,), (0,)))
        + dot(oth[:, :half], grad_query[half:], ((1,), (0,)))
        + dot(kv_all, grad_kv, ((1,), (0,)))
    ).astype(BF16)
    row_part = split3(jnp.sum(terms.astype(F32) * unit_b, axis=0)).astype(BF16)
    extra = jnp.broadcast_to(jnp.pad(row_part, ((0, 13), (0, 0)))[None], (8, 16, row_count))
    back = lax.all_to_all(jnp.concatenate([for_heads(terms), extra], axis=1), HEAD, 0, 0)

    attn_share = unpadded(jnp.sum(attn.astype(F32), axis=0), share)
    token_share = lax.dynamic_slice_in_dim(tokens.T, start, share, 0).astype(F32)
    layer_out = (token_share + attn_share + gate[None, :] * steer_rows).astype(BF16)
    back = jnp.sum(back.astype(F32), axis=0)
    gain_share = lax.dynamic_slice_in_dim(gain, start, share, 0)[:, None]
    gate_share = lax.dynamic_slice_in_dim(w_gate, start, share, 0)[:, None]
    total = unpadded(back[: 8 * PAD], share) + grad_logit[None, :] * gate_share
    gate_total = jnp.sum(unit * (gain * w_gate)[:, None], axis=0)
    row_total = jnp.sum(back[8 * PAD : 8 * PAD + 3], axis=0) + grad_logit * gate_total
    unit_share = token_share * inverse
    scaled = total * gain_share
    grad_tokens = (
        grad_share + inverse * (scaled - unit_share * (row_total / model_width)[None, :])
    ).astype(BF16)
    return (layer_out.T, grad_tokens.T, steer_grad)


def solution(mesh):
    split = Mesh(mesh.devices.reshape(4, 8, 2, 4, 2), SEQ + HEAD)
    placed = (
        P(SEQ, None),
        P(),
        P(SEQ, HEAD),
        P(SEQ, HEAD),
        P(SEQ, HEAD),
        P(SEQ, HEAD),
        P(),
        P(),
        P(SEQ),
        P(SEQ),
        P(SEQ, None),
    )
    return jax.shard_map(
        shards,
        mesh=split,
        in_specs=placed,
        out_specs=(P(SEQ, HEAD), P(SEQ, HEAD), P(None, HEAD)),
        check_vma=False,
    )
```

```python
import jax
import jax.numpy as jnp
from jax import lax
from jax.experimental import pallas as pl
from jax.experimental.pallas import tpu as pltpu
from jax.sharding import Mesh, PartitionSpec as P

HD = 64
WIN = 128
EPSILON = 1e-05
HIGHEST = lax.Precision.HIGHEST
SEQ = ("zh", "y", "core")
HEAD = ("x", "zl")
F32 = jnp.float32
BF16 = jnp.bfloat16
PAD = 48


def shifted(value, by):
    count = lax.axis_size(SEQ)
    pairs = [(i, i + by) for i in range(count) if 0 <= i + by < count]
    return lax.ppermute(value, SEQ, pairs)


def gathered(value, axes):
    count = lax.axis_size(axes)
    spread = jnp.broadcast_to(value[None], (count,) + value.shape)
    return lax.all_to_all(spread, axes, 0, 0)


def dot(left, right, dims, **kw):
    return lax.dot_general(left, right, (dims, ((), ())), preferred_element_type=F32, **kw)


def blocked(rows):
    width = rows.shape[-1]
    parts = rows.reshape(4, 8, 2, -1, width).transpose(1, 0, 2, 3, 4)
    parts = jnp.pad(parts, ((0, 0), (0, 0), (0, 0), (0, PAD - parts.shape[3]), (0, 0)))
    return parts.reshape(-1, width)


def unpadded(rows, row_count):
    width = rows.shape[-1]
    return rows.reshape(8, PAD, width)[:, : row_count // 8].reshape(row_count, width)


def mm(left, right, left_dim, right_dim):
    dims = (((left_dim,), (right_dim,)), ((), ()))
    return lax.dot_general(left, right, dims, preferred_element_type=F32)


def own_kernel(weight, normed, grads, query, grad):
    half = weight.shape[1] // 2
    query[...] = mm(weight[:, :half], normed[...], 0, 0).astype(BF16)
    grad[...] = mm(weight[:, half:], grads[...], 0, 0).astype(BF16)


def attend_kernel(
    oth, normed, grads, q_own, g_own, kv, halo, mask, mixed, grad_query, grad_halo, grad_kv
):
    half = oth.shape[1] // 2
    q_oth = mm(oth[:, :half], normed[...], 0, 0).astype(BF16)
    g_oth = mm(oth[:, half:], grads[...], 0, 0).astype(BF16)
    keys = jnp.concatenate([halo[:HD, :], kv[:HD, :]], axis=1)
    values = jnp.concatenate([halo[HD:, :], kv[HD:, :]], axis=1)
    allowed = mask[...] > 0.0
    grad_keys = jnp.zeros(keys.shape, F32)
    grad_values = jnp.zeros(keys.shape, F32)
    for head in range(8):
        low = head % 4 * HD
        rows = pl.ds(head * HD, HD)
        query = q_own[low : low + HD, :] if head < 4 else q_oth[low : low + HD]
        grad = g_own[low : low + HD, :] if head < 4 else g_oth[low : low + HD]
        scores = mm(keys, query, 0, 0) * HD**-0.5
        scores = jnp.where(allowed, scores, -jnp.inf)
        raised = jnp.exp(scores - jnp.max(scores, axis=0, keepdims=True))
        prob = raised / jnp.sum(raised, axis=0, keepdims=True)
        prob_b = prob.astype(BF16)
        mixed[rows, :] = mm(values, prob_b, 1, 0).astype(BF16)
        grad_values += mm(grad, prob_b, 1, 1)
        grad_prob = mm(values, grad, 0, 0)
        delta = jnp.sum(prob * grad_prob, axis=0, keepdims=True)
        grad_scores = (prob * (grad_prob - delta) * HD**-0.5).astype(BF16)
        grad_query[rows, :] = mm(keys, grad_scores, 1, 0).astype(BF16)
        grad_keys += mm(query, grad_scores, 1, 1)
    grad_halo[:HD, :] = grad_keys[:, :WIN].astype(BF16)
    grad_halo[HD:, :] = grad_values[:, :WIN].astype(BF16)
    grad_kv[:HD, :] = grad_keys[:, WIN:]
    grad_kv[HD:, :] = grad_values[:, WIN:]


def chunks():
    for group in range(8):
        for part in range(4):
            row = ((group % 2 * 4 + part) * 4 + group // 2) * 2 * PAD
            yield group, part * 2 * PAD, row


def out_kernel(own, oth, mixed, blocks):
    half = own.shape[1] // 2
    for group, place, row in chunks():
        term = mm(own[row : row + 2 * PAD, half:], mixed[:half, :], 1, 0)
        term = term + mm(oth[row : row + 2 * PAD, half:], mixed[half:, :], 1, 0)
        blocks[group, place : place + 2 * PAD, :] = term.astype(BF16)


def back_kernel(own, oth, kv_all, normed, grad_query, grad_kv, returned, blocks):
    half = own.shape[1] // 2
    tokens_here = grad_kv.shape[1]
    kv_grad = (grad_kv[...] + returned[...].astype(F32)).astype(BF16)
    rows = jnp.zeros((2 * PAD, tokens_here), F32)
    for group, place, row in chunks():
        term = mm(own[row : row + 2 * PAD, :half], grad_query[:half, :], 1, 0)
        term = term + mm(oth[row : row + 2 * PAD, :half], grad_query[half:, :], 1, 0)
        term = term + mm(kv_all[row : row + 2 * PAD, :], kv_grad, 1, 0)
        term = term.astype(BF16)
        blocks[group, place : place + 2 * PAD, :] = term
        rows += term.astype(F32) * normed[row : row + 2 * PAD, :].astype(F32)
    total = jnp.sum(rows, axis=0, keepdims=True)
    high = total.astype(BF16).astype(F32)
    mid = (total - high).astype(BF16).astype(F32)
    low = total - high - mid
    line = lax.broadcasted_iota(jnp.int32, (16, tokens_here), 0)
    extra = jnp.where(line == 0, high, jnp.where(line == 1, mid, jnp.where(line == 2, low, 0.0)))
    for group in range(8):
        blocks[group, 8 * PAD :, :] = extra.astype(BF16)


def call(kernel, outs, *args):
    size = sum(a.size * a.dtype.itemsize for a in jax.tree.leaves((args, outs)))
    return pl.pallas_call(
        kernel,
        out_shape=outs,
        compiler_params=pltpu.CompilerParams(vmem_limit_bytes=40 * 2**20),
        cost_estimate=pl.CostEstimate(flops=10**8, bytes_accessed=size, transcendentals=0),
    )(*args)


def shards(
    tokens,
    gain,
    w_query,
    w_key,
    w_value,
    w_out,
    w_gate,
    steering,
    segment_ids,
    steer_index,
    grad_out,
):
    row_count, model_width = tokens.shape
    share = model_width // 8
    start = lax.axis_index(HEAD) * share

    padded = lambda w: jnp.pad(w, ((0, PAD - w.shape[0]), (0, 0)))
    half = w_query.shape[1] // 2
    query_w, out_w = padded(w_query), padded(w_out)
    w_kv = padded(jnp.concatenate([w_key, w_value], axis=1))
    w_kv = w_kv.reshape(2, 6, 4 * 2 * HD)

    def pair(c):
        columns = slice(c * half, (c + 1) * half)
        wide = jnp.concatenate([query_w[:, columns], out_w[:, columns]], axis=1)
        return jnp.concatenate([wide, w_kv[c], jnp.zeros((2, 2 * half), BF16)], axis=0)

    sent = jnp.stack([pair(0), pair(1)] * 4)
    near = lax.all_to_all(sent, ("zh", "core"), 0, 0)
    own = lax.all_gather(near[:, :PAD], "y", axis=0, tiled=True).reshape(-1, 2 * half)
    kv_near = near[:, PAD : PAD + 6].reshape(8, PAD // 2, 2 * HD)
    kv_near = lax.all_gather(kv_near, "y", axis=0, tiled=True)
    kv_all = lax.all_gather(kv_near, "core", axis=1, tiled=True).reshape(-1, 2 * HD)

    tok = tokens.T.astype(F32)
    inverse = lax.rsqrt(jnp.mean(tok * tok, axis=0, keepdims=True) + EPSILON)
    unit = tok * inverse
    normed = (unit * gain[:, None]).astype(BF16)
    normed_b = blocked(normed)
    grad_t = grad_out.T
    grad_b = blocked(grad_t)
    gate = jax.nn.sigmoid(jnp.sum(normed.astype(F32) * w_gate[:, None], axis=0))
    one_hot = steer_index[None, :] == lax.broadcasted_iota(jnp.int32, (16, row_count), 0)
    products = dot(steering, grad_t, ((1,), (0,)))
    grad_logit = gate * (1.0 - gate) * jnp.sum(jnp.where(one_hot, products, 0.0), axis=0)
    steer_share = lax.dynamic_slice_in_dim(steering, start, share, 1)
    steer_rows = dot(steer_share, one_hot.astype(BF16), ((0,), (0,)))
    grad_share = lax.dynamic_slice_in_dim(grad_t, start, share, 0).astype(F32)
    steer_part = dot(
        one_hot.astype(F32), gate[None, :] * grad_share, ((1,), (1,)), precision=HIGHEST
    )
    steer_near = jnp.sum(gathered(steer_part, ("zh", "core")), axis=0)
    steer_grad = jnp.sum(gathered(steer_near, ("y",)), axis=0)

    halo_seg = shifted(segment_ids, 1)
    halo_seg = jnp.where(lax.axis_index(SEQ) > 0, halo_seg, -1)
    kv = dot(kv_all, normed_b, ((0,), (0,))).astype(BF16)
    halo = shifted(kv, 1)
    wide_seg = jnp.concatenate([halo_seg, segment_ids])
    key_pos = lax.broadcasted_iota(jnp.int32, (2 * row_count, row_count), 0) - WIN
    query_pos = lax.broadcasted_iota(jnp.int32, (2 * row_count, row_count), 1)
    distance = query_pos - key_pos
    mask = (distance >= 0) & (distance < WIN) & (wide_seg[:, None] == segment_ids[None, :])
    mask = mask.astype(F32)
    own, halo, mask, steer_grad, normed_b, grad_b, kv, kv_all = lax.optimization_barrier(
        (own, halo, mask, steer_grad, normed_b, grad_b, kv, kv_all)
    )
    oth = lax.ppermute(own, "core", [(0, 1), (1, 0)])
    like = jax.ShapeDtypeStruct
    thin = like((half, row_count), BF16)
    q_own, g_own = call(own_kernel, (thin, thin), own, normed_b, grad_b)
    mixed, grad_query, grad_halo, grad_kv = call(
        attend_kernel,
        (
            like((2 * half, row_count), BF16),
            like((2 * half, row_count), BF16),
            like((2 * HD, row_count), BF16),
            like((2 * HD, row_count), F32),
        ),
        *(oth, normed_b, grad_b, q_own, g_own, kv, halo, mask),
    )
    returned = shifted(grad_halo, -1)
    blocks = call(out_kernel, like((8, 8 * PAD, row_count), BF16), own, oth, mixed)
    attn = lax.all_to_all(blocks, HEAD, 0, 0)
    blocks, grad_query = lax.optimization_barrier((blocks, grad_query))
    back = call(
        back_kernel,
        like((8, 8 * PAD + 16, row_count), BF16),
        *(own, oth, kv_all, normed_b, grad_query, grad_kv, returned),
    )
    back = lax.all_to_all(back, HEAD, 0, 0)

    attn_share = unpadded(jnp.sum(attn.astype(F32), axis=0), share)
    token_share = lax.dynamic_slice_in_dim(tokens.T, start, share, 0).astype(F32)
    layer_out = (token_share + attn_share + gate[None, :] * steer_rows).astype(BF16)
    back = jnp.sum(back.astype(F32), axis=0)
    gain_share = lax.dynamic_slice_in_dim(gain, start, share, 0)[:, None]
    gate_share = lax.dynamic_slice_in_dim(w_gate, start, share, 0)[:, None]
    total = unpadded(back[: 8 * PAD], share) + grad_logit[None, :] * gate_share
    gate_total = jnp.sum(unit * (gain * w_gate)[:, None], axis=0)
    row_total = jnp.sum(back[8 * PAD : 8 * PAD + 3], axis=0) + grad_logit * gate_total
    unit_share = token_share * inverse
    scaled = total * gain_share
    grad_tokens = (
        grad_share + inverse * (scaled - unit_share * (row_total / model_width)[None, :])
    ).astype(BF16)
    return (layer_out.T, grad_tokens.T, steer_grad)


def solution(mesh):
    split = Mesh(mesh.devices.reshape(4, 8, 2, 4, 2), SEQ + HEAD)
    placed = (
        P(SEQ, None),
        P(),
        P(SEQ, HEAD),
        P(SEQ, HEAD),
        P(SEQ, HEAD),
        P(SEQ, HEAD),
        P(),
        P(),
        P(SEQ),
        P(SEQ),
        P(SEQ, None),
    )
    return jax.shard_map(
        shards,
        mesh=split,
        in_specs=placed,
        out_specs=(P(SEQ, HEAD), P(SEQ, HEAD), P(None, HEAD)),
        check_vma=False,
    )
```

```python
import functools

import jax
import jax.numpy as jnp
from jax import lax
from jax.experimental import pallas as pl
from jax.experimental.pallas import tpu as pltpu
from jax.sharding import Mesh, PartitionSpec as P

HD = 64
WIN = 128
EPSILON = 1e-05
HIGHEST = lax.Precision.HIGHEST
SEQ = ("zh", "y", "core")
HEAD = ("x", "zl")
F32 = jnp.float32
BF16 = jnp.bfloat16
PAD = 48


def shifted(value, by):
    count = lax.axis_size(SEQ)
    pairs = [(i, i + by) for i in range(count) if 0 <= i + by < count]
    return lax.ppermute(value, SEQ, pairs)


def gathered(value, axes):
    count = lax.axis_size(axes)
    spread = jnp.broadcast_to(value[None], (count,) + value.shape)
    return lax.all_to_all(spread, axes, 0, 0)


def dot(left, right, dims, **kw):
    return lax.dot_general(left, right, (dims, ((), ())), preferred_element_type=F32, **kw)


def blocked(rows):
    width = rows.shape[-1]
    parts = rows.reshape(4, 8, 2, -1, width).transpose(1, 0, 2, 3, 4)
    parts = jnp.pad(parts, ((0, 0), (0, 0), (0, 0), (0, PAD - parts.shape[3]), (0, 0)))
    return parts.reshape(-1, width)


def unpadded(rows, row_count):
    width = rows.shape[-1]
    return rows.reshape(8, PAD, width)[:, : row_count // 8].reshape(row_count, width)


def mm(left, right, left_dim, right_dim):
    dims = (((left_dim,), (right_dim,)), ((), ()))
    return lax.dot_general(left, right, dims, preferred_element_type=F32)


def attend_kernel(last, weight, normed, grads, kv, halo, mask, *refs):
    if last:
        grad_first, mixed, grad_query, grad_halo, grad_kv = refs
        grad_keys, grad_values = grad_first[:HD, :], grad_first[HD:, :]
    else:
        mixed, grad_query, grad_kv = refs
        grad_keys = grad_values = jnp.zeros((HD, 2 * WIN), F32)
    half = weight.shape[1] // 2
    query_all = mm(weight[:, :half], normed[...], 0, 0).astype(BF16)
    grad_all = mm(weight[:, half:], grads[...], 0, 0).astype(BF16)
    keys = jnp.concatenate([halo[:HD, :], kv[:HD, :]], axis=1)
    values = jnp.concatenate([halo[HD:, :], kv[HD:, :]], axis=1)
    allowed = mask[...] > 0.0
    for head in range(4):
        rows = slice(head * HD, (head + 1) * HD)
        query, grad = query_all[rows], grad_all[rows]
        scores = mm(keys, query, 0, 0) * HD**-0.5
        scores = jnp.where(allowed, scores, -jnp.inf)
        raised = jnp.exp(scores - jnp.max(scores, axis=0, keepdims=True))
        prob = raised / jnp.sum(raised, axis=0, keepdims=True)
        prob_b = prob.astype(BF16)
        mixed[rows, :] = mm(values, prob_b, 1, 0).astype(BF16)
        grad_values += mm(grad, prob_b, 1, 1)
        grad_prob = mm(values, grad, 0, 0)
        delta = jnp.sum(prob * grad_prob, axis=0, keepdims=True)
        grad_scores = (prob * (grad_prob - delta) * HD**-0.5).astype(BF16)
        grad_query[rows, :] = mm(keys, grad_scores, 1, 0).astype(BF16)
        grad_keys += mm(query, grad_scores, 1, 1)
    if last:
        grad_halo[:HD, :] = grad_keys[:, :WIN].astype(BF16)
        grad_halo[HD:, :] = grad_values[:, :WIN].astype(BF16)
        grad_kv[:HD, :] = grad_keys[:, WIN:]
        grad_kv[HD:, :] = grad_values[:, WIN:]
    else:
        grad_kv[:HD, :] = grad_keys
        grad_kv[HD:, :] = grad_values


def chunks():
    for group in range(8):
        for part in range(4):
            row = ((group % 2 * 4 + part) * 4 + group // 2) * 2 * PAD
            yield group, part * 2 * PAD, row


def out_kernel(own, oth, m_own, m_oth, blocks):
    half = own.shape[1] // 2
    for group, place, row in chunks():
        term = mm(own[row : row + 2 * PAD, half:], m_own[...], 1, 0)
        term = term + mm(oth[row : row + 2 * PAD, half:], m_oth[...], 1, 0)
        blocks[group, place : place + 2 * PAD, :] = term.astype(BF16)


def back_kernel(own, oth, kv_all, normed, d_own, d_oth, grad_kv, returned, blocks):
    half = own.shape[1] // 2
    tokens_here = grad_kv.shape[1]
    kv_grad = (grad_kv[...] + returned[...].astype(F32)).astype(BF16)
    rows = jnp.zeros((2 * PAD, tokens_here), F32)
    for group, place, row in chunks():
        term = mm(own[row : row + 2 * PAD, :half], d_own[...], 1, 0)
        term = term + mm(oth[row : row + 2 * PAD, :half], d_oth[...], 1, 0)
        term = term + mm(kv_all[row : row + 2 * PAD, :], kv_grad, 1, 0)
        term = term.astype(BF16)
        blocks[group, place : place + 2 * PAD, :] = term
        rows += term.astype(F32) * normed[row : row + 2 * PAD, :].astype(F32)
    total = jnp.sum(rows, axis=0, keepdims=True)
    high = total.astype(BF16).astype(F32)
    mid = (total - high).astype(BF16).astype(F32)
    low = total - high - mid
    line = lax.broadcasted_iota(jnp.int32, (16, tokens_here), 0)
    extra = jnp.where(line == 0, high, jnp.where(line == 1, mid, jnp.where(line == 2, low, 0.0)))
    for group in range(8):
        blocks[group, 8 * PAD :, :] = extra.astype(BF16)


def call(kernel, outs, *args):
    size = sum(a.size * a.dtype.itemsize for a in jax.tree.leaves((args, outs)))
    return pl.pallas_call(
        kernel,
        out_shape=outs,
        compiler_params=pltpu.CompilerParams(vmem_limit_bytes=12 * 2**20),
        cost_estimate=pl.CostEstimate(flops=10**8, bytes_accessed=size, transcendentals=0),
    )(*args)


def shards(
    tokens,
    gain,
    w_query,
    w_key,
    w_value,
    w_out,
    w_gate,
    steering,
    segment_ids,
    steer_index,
    grad_out,
):
    row_count, model_width = tokens.shape
    share = model_width // 8
    start = lax.axis_index(HEAD) * share

    padded = lambda w: jnp.pad(w, ((0, PAD - w.shape[0]), (0, 0)))
    half = w_query.shape[1] // 2
    query_w, out_w = padded(w_query), padded(w_out)
    w_kv = padded(jnp.concatenate([w_key, w_value], axis=1))
    w_kv = w_kv.reshape(2, 6, 4 * 2 * HD)

    def pair(c):
        columns = slice(c * half, (c + 1) * half)
        wide = jnp.concatenate([query_w[:, columns], out_w[:, columns]], axis=1)
        return jnp.concatenate([wide, w_kv[c], jnp.zeros((2, 2 * half), BF16)], axis=0)

    sent = jnp.stack([pair(0), pair(1)] * 4)
    near = lax.all_to_all(sent, ("zh", "core"), 0, 0)
    own = lax.all_gather(near[:, :PAD], "y", axis=0, tiled=True).reshape(-1, 2 * half)
    kv_near = near[:, PAD : PAD + 6].reshape(8, PAD // 2, 2 * HD)
    kv_near = gathered(kv_near, ("y",)).reshape(64, PAD // 2, 2 * HD)
    kv_all = lax.all_gather(kv_near, "core", axis=1, tiled=True).reshape(-1, 2 * HD)

    tok = tokens.T.astype(F32)
    inverse = lax.rsqrt(jnp.mean(tok * tok, axis=0, keepdims=True) + EPSILON)
    unit = tok * inverse
    normed = (unit * gain[:, None]).astype(BF16)
    normed_b = blocked(normed)
    grad_t = grad_out.T
    grad_b = blocked(grad_t)
    gate = jax.nn.sigmoid(jnp.sum(normed.astype(F32) * w_gate[:, None], axis=0))
    one_hot = steer_index[None, :] == lax.broadcasted_iota(jnp.int32, (16, row_count), 0)
    products = dot(steering, grad_t, ((1,), (0,)))
    grad_logit = gate * (1.0 - gate) * jnp.sum(jnp.where(one_hot, products, 0.0), axis=0)
    steer_share = lax.dynamic_slice_in_dim(steering, start, share, 1)
    steer_rows = dot(steer_share, one_hot.astype(BF16), ((0,), (0,)))
    grad_share = lax.dynamic_slice_in_dim(grad_t, start, share, 0).astype(F32)
    steer_part = dot(
        one_hot.astype(F32), gate[None, :] * grad_share, ((1,), (1,)), precision=HIGHEST
    )
    steer_grad = steer_part
    for axis, step in (("core", 1), ("zh", 1), ("zh", 2), ("y", 1), ("y", 2), ("y", 4)):
        pairs = [(i, i ^ step) for i in range(lax.axis_size(axis))]
        steer_grad = steer_grad + lax.ppermute(steer_grad, axis, pairs)

    halo_seg = shifted(segment_ids, 1)
    halo_seg = jnp.where(lax.axis_index(SEQ) > 0, halo_seg, -1)
    kv = dot(kv_all, normed_b, ((0,), (0,))).astype(BF16)
    halo = shifted(kv, 1)
    wide_seg = jnp.concatenate([halo_seg, segment_ids])
    key_pos = lax.broadcasted_iota(jnp.int32, (2 * row_count, row_count), 0) - WIN
    query_pos = lax.broadcasted_iota(jnp.int32, (2 * row_count, row_count), 1)
    distance = query_pos - key_pos
    mask = (distance >= 0) & (distance < WIN) & (wide_seg[:, None] == segment_ids[None, :])
    mask = mask.astype(F32)
    own, halo, mask, steer_grad, normed_b, grad_b, kv, kv_all = lax.optimization_barrier(
        (own, halo, mask, steer_grad, normed_b, grad_b, kv, kv_all)
    )
    oth = lax.ppermute(own, "core", [(0, 1), (1, 0)])
    like = jax.ShapeDtypeStruct
    thin = like((half, row_count), BF16)
    m_own, d_own, grad_first = call(
        functools.partial(attend_kernel, False),
        (thin, thin, like((2 * HD, 2 * row_count), F32)),
        *(own, normed_b, grad_b, kv, halo, mask),
    )
    m_oth, d_oth, grad_halo, grad_kv = call(
        functools.partial(attend_kernel, True),
        (thin, thin, like((2 * HD, row_count), BF16), like((2 * HD, row_count), F32)),
        *(oth, normed_b, grad_b, kv, halo, mask, grad_first),
    )
    returned = shifted(grad_halo, -1)
    blocks = call(out_kernel, like((8, 8 * PAD, row_count), BF16), own, oth, m_own, m_oth)
    attn = lax.all_to_all(blocks, HEAD, 0, 0)
    blocks, d_own = lax.optimization_barrier((blocks, d_own))
    back = call(
        back_kernel,
        like((8, 8 * PAD + 16, row_count), BF16),
        *(own, oth, kv_all, normed_b, d_own, d_oth, grad_kv, returned),
    )
    back = lax.all_to_all(back, HEAD, 0, 0)

    attn_share = unpadded(jnp.sum(attn.astype(F32), axis=0), share)
    token_share = lax.dynamic_slice_in_dim(tokens.T, start, share, 0).astype(F32)
    layer_out = (token_share + attn_share + gate[None, :] * steer_rows).astype(BF16)
    back = jnp.sum(back.astype(F32), axis=0)
    gain_share = lax.dynamic_slice_in_dim(gain, start, share, 0)[:, None]
    gate_share = lax.dynamic_slice_in_dim(w_gate, start, share, 0)[:, None]
    total = unpadded(back[: 8 * PAD], share) + grad_logit[None, :] * gate_share
    gate_total = jnp.sum(unit * (gain * w_gate)[:, None], axis=0)
    row_total = jnp.sum(back[8 * PAD : 8 * PAD + 3], axis=0) + grad_logit * gate_total
    unit_share = token_share * inverse
    scaled = total * gain_share
    grad_tokens = (
        grad_share + inverse * (scaled - unit_share * (row_total / model_width)[None, :])
    ).astype(BF16)
    return (layer_out.T, grad_tokens.T, steer_grad)


def solution(mesh):
    split = Mesh(mesh.devices.reshape(4, 8, 2, 4, 2), SEQ + HEAD)
    placed = (
        P(SEQ, None),
        P(),
        P(SEQ, HEAD),
        P(SEQ, HEAD),
        P(SEQ, HEAD),
        P(SEQ, HEAD),
        P(),
        P(),
        P(SEQ),
        P(SEQ),
        P(SEQ, None),
    )
    return jax.shard_map(
        shards,
        mesh=split,
        in_specs=placed,
        out_specs=(P(SEQ, HEAD), P(SEQ, HEAD), P(None, HEAD)),
        check_vma=False,
    )
```

```python
import functools

import jax
import jax.numpy as jnp
from jax import lax
from jax.experimental import pallas as pl
from jax.experimental.pallas import tpu as pltpu
from jax.sharding import Mesh, PartitionSpec as P

HD = 64
WIN = 128
EPSILON = 1e-05
HIGHEST = lax.Precision.HIGHEST
SEQ = ("zh", "y", "core")
HEAD = ("x", "zl")
F32 = jnp.float32
BF16 = jnp.bfloat16
PAD = 48


def shifted(value, by):
    count = lax.axis_size(SEQ)
    pairs = [(i, i + by) for i in range(count) if 0 <= i + by < count]
    return lax.ppermute(value, SEQ, pairs)


def gathered(value, axes):
    count = lax.axis_size(axes)
    spread = jnp.broadcast_to(value[None], (count,) + value.shape)
    return lax.all_to_all(spread, axes, 0, 0)


def dot(left, right, dims, **kw):
    return lax.dot_general(left, right, (dims, ((), ())), preferred_element_type=F32, **kw)


def blocked(rows):
    width = rows.shape[-1]
    parts = rows.reshape(4, 8, 2, -1, width).transpose(1, 2, 0, 3, 4)
    parts = jnp.pad(parts, ((0, 0), (0, 0), (0, 0), (0, PAD - parts.shape[3]), (0, 0)))
    return parts.reshape(-1, width)


def unpadded(rows, row_count):
    width = rows.shape[-1]
    return rows.reshape(8, PAD, width)[:, : row_count // 8].reshape(row_count, width)


def mm(left, right, left_dim, right_dim):
    dims = (((left_dim,), (right_dim,)), ((), ()))
    return lax.dot_general(left, right, dims, preferred_element_type=F32)


def pack_kernel(w_query, w_out, w_key, w_value, out):
    rows = w_query.shape[0]
    width = w_query.shape[1]
    out[...] = jnp.zeros(out.shape, BF16)
    for place in range(out.shape[0]):
        out[place, :rows, :width] = w_query[...]
        out[place, :rows, width : 2 * width] = w_out[...]
        out[place, :rows, 2 * width : 2 * width + HD] = w_key[...]
        out[place, :rows, 2 * width + HD :] = w_value[...]


def pieces():
    for group in range(8):
        for part in range(8):
            row = ((group % 2 * 8 + part) * 4 + group // 2) * PAD
            yield group, part * PAD, row


def attend_kernel(
    w_hbm, x_hbm, g_hbm, kv, halo, mask, blocks_hbm, grad_query, grad_halo, grad_kv, *scratch
):
    weight, normed, grads, blocks, sems, out_sems = scratch
    count = sems.shape[0]
    size = weight.shape[0] // count
    width = weight.shape[1] // 2
    copies = []
    for step in range(count):
        rows = pl.ds(step * size, size)
        trio = ((w_hbm, weight), (x_hbm, normed), (g_hbm, grads))
        copies.append(
            [
                pltpu.make_async_copy(a.at[rows, :], b.at[rows, :], sems.at[step, k])
                for k, (a, b) in enumerate(trio)
            ]
        )
        for copy in copies[-1]:
            copy.start()
    keys = jnp.concatenate([halo[:HD, :], kv[:HD, :]], axis=1)
    values = jnp.concatenate([halo[HD:, :], kv[HD:, :]], axis=1)
    allowed = mask[...] > 0.0
    query_sum = jnp.zeros((width, WIN), F32)
    grad_sum = jnp.zeros((width, WIN), F32)
    for step in range(count):
        for copy in copies[step]:
            copy.wait()
        rows = slice(step * size, (step + 1) * size)
        query_sum += mm(weight[rows, :width], normed[rows, :], 0, 0)
        grad_sum += mm(weight[rows, width:], grads[rows, :], 0, 0)
    query_all = query_sum.astype(BF16)
    grad_all = grad_sum.astype(BF16)
    grad_keys = grad_values = jnp.zeros((HD, 2 * WIN), F32)
    mixed = []
    for head in range(8):
        rows = slice(head * HD, (head + 1) * HD)
        query, grad = query_all[rows], grad_all[rows]
        scores = mm(keys, query, 0, 0) * HD**-0.5
        scores = jnp.where(allowed, scores, -jnp.inf)
        raised = jnp.exp(scores - jnp.max(scores, axis=0, keepdims=True))
        prob = raised / jnp.sum(raised, axis=0, keepdims=True)
        prob_b = prob.astype(BF16)
        mixed.append(mm(values, prob_b, 1, 0).astype(BF16))
        grad_values += mm(grad, prob_b, 1, 1)
        grad_prob = mm(values, grad, 0, 0)
        delta = jnp.sum(prob * grad_prob, axis=0, keepdims=True)
        grad_scores = (prob * (grad_prob - delta) * HD**-0.5).astype(BF16)
        grad_query[rows, :] = mm(keys, grad_scores, 1, 0).astype(BF16)
        grad_keys += mm(query, grad_scores, 1, 1)
    grad_halo[:HD, :] = grad_keys[:, :WIN].astype(BF16)
    grad_halo[HD:, :] = grad_values[:, :WIN].astype(BF16)
    grad_kv[:HD, :] = grad_keys[:, WIN:]
    grad_kv[HD:, :] = grad_values[:, WIN:]
    mixed = jnp.concatenate(mixed, axis=0)
    sent = []
    for group, place, row in pieces():
        term = mm(weight[row : row + PAD, width:], mixed, 1, 0)
        blocks[group, place : place + PAD, :] = term.astype(BF16)
        if place == 7 * PAD:
            copy = pltpu.make_async_copy(
                blocks.at[group], blocks_hbm.at[group], out_sems.at[group]
            )
            copy.start()
            sent.append(copy)
    for copy in sent:
        copy.wait()


def back_kernel(w_hbm, kv_hbm, x_hbm, grad_query, grad_kv, returned, blocks_hbm, *scratch):
    weight, kv_all, normed, blocks, sems, out_sems = scratch
    width = weight.shape[1]
    size = weight.shape[0] // 2
    copies = []
    for step in range(2):
        rows = pl.ds(step * size, size)
        copies.append(
            [
                pltpu.make_async_copy(
                    w_hbm.at[rows, pl.ds(0, width)], weight.at[rows, :], sems.at[step, 0]
                ),
                pltpu.make_async_copy(kv_hbm.at[rows, :], kv_all.at[rows, :], sems.at[step, 1]),
                pltpu.make_async_copy(x_hbm.at[rows, :], normed.at[rows, :], sems.at[step, 2]),
            ]
        )
        for copy in copies[-1]:
            copy.start()
    tokens_here = grad_kv.shape[1]
    kv_grad = (grad_kv[...] + returned[...].astype(F32)).astype(BF16)
    rows_sum = jnp.zeros((PAD, tokens_here), F32)
    ordered = sorted(pieces(), key=lambda piece: piece[2] >= size)
    ready = 0
    for group, place, row in ordered:
        if ready < 1 + (row >= size):
            for copy in copies[ready]:
                copy.wait()
            ready += 1
        term = mm(weight[row : row + PAD, :], grad_query[...], 1, 0)
        term = term + mm(kv_all[row : row + PAD, :], kv_grad, 1, 0)
        term = term.astype(BF16)
        blocks[group, place : place + PAD, :] = term
        rows_sum += term.astype(F32) * normed[row : row + PAD, :].astype(F32)
    total = jnp.sum(rows_sum, axis=0, keepdims=True)
    high = total.astype(BF16).astype(F32)
    mid = (total - high).astype(BF16).astype(F32)
    low = total - high - mid
    line = lax.broadcasted_iota(jnp.int32, (16, tokens_here), 0)
    extra = jnp.where(line == 0, high, jnp.where(line == 1, mid, jnp.where(line == 2, low, 0.0)))
    sent = []
    for group in range(8):
        blocks[group, 8 * PAD :, :] = extra.astype(BF16)
        copy = pltpu.make_async_copy(blocks.at[group], blocks_hbm.at[group], out_sems.at[group])
        copy.start()
        sent.append(copy)
    for copy in sent:
        copy.wait()


ANY = pl.BlockSpec(memory_space=pltpu.MemorySpace.HBM)
FULL = pl.BlockSpec(memory_space=pltpu.MemorySpace.VMEM)


def call(kernel, outs, in_specs, out_specs, scratch, *args):
    size = sum(a.size * a.dtype.itemsize for a in jax.tree.leaves((args, outs)))
    return pl.pallas_call(
        kernel,
        out_shape=outs,
        in_specs=in_specs,
        out_specs=out_specs,
        scratch_shapes=scratch,
        compiler_params=pltpu.CompilerParams(vmem_limit_bytes=58 * 2**20),
        cost_estimate=pl.CostEstimate(flops=10**8, bytes_accessed=size, transcendentals=0),
    )(*args)


def shards(
    tokens,
    gain,
    w_query,
    w_key,
    w_value,
    w_out,
    w_gate,
    steering,
    segment_ids,
    steer_index,
    grad_out,
):
    row_count, model_width = tokens.shape
    share = model_width // 8
    start = lax.axis_index(HEAD) * share

    width = w_query.shape[1]
    like = jax.ShapeDtypeStruct
    sent = call(
        pack_kernel,
        like((4, PAD, 2 * width + 2 * HD), BF16),
        [FULL] * 4,
        FULL,
        [],
        *(w_query, w_out, w_key, w_value),
    )
    near = lax.all_to_all(sent, "zh", 0, 0)
    whole = lax.all_gather(near[:, :, : 2 * width], ("y", "core"), axis=0, tiled=True)
    whole = whole.reshape(-1, 2 * width)
    kv_near = gathered(near[:, :, 2 * width :], ("y",))
    kv_all = lax.all_gather(kv_near[:, None], "core", axis=1, tiled=True).reshape(-1, 2 * HD)

    tok = tokens.T.astype(F32)
    inverse = lax.rsqrt(jnp.mean(tok * tok, axis=0, keepdims=True) + EPSILON)
    unit = tok * inverse
    normed = (unit * gain[:, None]).astype(BF16)
    normed_b = blocked(normed)
    grad_t = grad_out.T
    grad_b = blocked(grad_t)
    gate = jax.nn.sigmoid(jnp.sum(normed.astype(F32) * w_gate[:, None], axis=0))
    one_hot = steer_index[None, :] == lax.broadcasted_iota(jnp.int32, (16, row_count), 0)
    products = dot(steering, grad_t, ((1,), (0,)))
    grad_logit = gate * (1.0 - gate) * jnp.sum(jnp.where(one_hot, products, 0.0), axis=0)
    steer_share = lax.dynamic_slice_in_dim(steering, start, share, 1)
    steer_rows = dot(steer_share, one_hot.astype(BF16), ((0,), (0,)))
    grad_share = lax.dynamic_slice_in_dim(grad_t, start, share, 0).astype(F32)
    steer_part = dot(
        one_hot.astype(F32), gate[None, :] * grad_share, ((1,), (1,)), precision=HIGHEST
    )

    def exchanged(value, *steps):
        for axis, step in steps:
            pairs = [(i, i ^ step) for i in range(lax.axis_size(axis))]
            value = value + lax.ppermute(value, axis, pairs)
        return value

    steer = exchanged(steer_part, ("core", 1), ("zh", 1))

    halo_seg = shifted(segment_ids, 1)
    halo_seg = jnp.where(lax.axis_index(SEQ) > 0, halo_seg, -1)
    kv = dot(kv_all, normed_b, ((0,), (0,))).astype(BF16)
    halo = shifted(kv, 1)
    wide_seg = jnp.concatenate([halo_seg, segment_ids])
    key_pos = lax.broadcasted_iota(jnp.int32, (2 * row_count, row_count), 0) - WIN
    query_pos = lax.broadcasted_iota(jnp.int32, (2 * row_count, row_count), 1)
    distance = query_pos - key_pos
    mask = (distance >= 0) & (distance < WIN) & (wide_seg[:, None] == segment_ids[None, :])
    mask = mask.astype(F32)
    steer, halo, kv, mask = lax.optimization_barrier((steer, halo, kv, mask))
    steer = exchanged(steer, ("zh", 2), ("y", 1))
    whole, halo, mask, steer, normed_b, grad_b, kv, kv_all = lax.optimization_barrier(
        (whole, halo, mask, steer, normed_b, grad_b, kv, kv_all)
    )
    total_rows = whole.shape[0]
    dma = pltpu.SemaphoreType.DMA
    blocks, grad_query, grad_halo, grad_kv = call(
        attend_kernel,
        (
            like((8, 8 * PAD, row_count), BF16),
            like((width, row_count), BF16),
            like((2 * HD, row_count), BF16),
            like((2 * HD, row_count), F32),
        ),
        [ANY, ANY, ANY, FULL, FULL, FULL],
        [ANY, FULL, FULL, FULL],
        [
            pltpu.VMEM((total_rows, 2 * width), BF16),
            pltpu.VMEM((total_rows, row_count), BF16),
            pltpu.VMEM((total_rows, row_count), BF16),
            pltpu.VMEM((8, 8 * PAD, row_count), BF16),
            dma((6, 3)),
            dma((8,)),
        ],
        *(whole, normed_b, grad_b, kv, halo, mask),
    )
    returned = shifted(grad_halo, -1)
    attn = lax.all_to_all(blocks, HEAD, 0, 0)
    back = call(
        back_kernel,
        like((8, 8 * PAD + 16, row_count), BF16),
        [ANY, ANY, ANY, FULL, FULL, FULL],
        ANY,
        [
            pltpu.VMEM((total_rows, width), BF16),
            pltpu.VMEM((total_rows, 2 * HD), BF16),
            pltpu.VMEM((total_rows, row_count), BF16),
            pltpu.VMEM((8, 8 * PAD + 16, row_count), BF16),
            dma((2, 3)),
            dma((8,)),
        ],
        *(whole, kv_all, normed_b, grad_query, grad_kv, returned),
    )
    steer, back = lax.optimization_barrier((steer, back))
    steer_grad = exchanged(steer, ("y", 2), ("y", 4))
    back = lax.all_to_all(back, HEAD, 0, 0)

    attn_share = unpadded(jnp.sum(attn.astype(F32), axis=0), share)
    token_share = lax.dynamic_slice_in_dim(tokens.T, start, share, 0).astype(F32)
    layer_out = (token_share + attn_share + gate[None, :] * steer_rows).astype(BF16)
    back = jnp.sum(back.astype(F32), axis=0)
    gain_share = lax.dynamic_slice_in_dim(gain, start, share, 0)[:, None]
    gate_share = lax.dynamic_slice_in_dim(w_gate, start, share, 0)[:, None]
    total = unpadded(back[: 8 * PAD], share) + grad_logit[None, :] * gate_share
    gate_total = jnp.sum(unit * (gain * w_gate)[:, None], axis=0)
    row_total = jnp.sum(back[8 * PAD : 8 * PAD + 3], axis=0) + grad_logit * gate_total
    unit_share = token_share * inverse
    scaled = total * gain_share
    grad_tokens = (
        grad_share + inverse * (scaled - unit_share * (row_total / model_width)[None, :])
    ).astype(BF16)
    return (layer_out.T, grad_tokens.T, steer_grad)


def solution(mesh):
    split = Mesh(mesh.devices.reshape(4, 8, 2, 4, 2), SEQ + HEAD)
    placed = (
        P(SEQ, None),
        P(),
        P(SEQ, HEAD),
        P(SEQ, HEAD),
        P(SEQ, HEAD),
        P(SEQ, HEAD),
        P(),
        P(),
        P(SEQ),
        P(SEQ),
        P(SEQ, None),
    )
    return jax.shard_map(
        shards,
        mesh=split,
        in_specs=placed,
        out_specs=(P(SEQ, HEAD), P(SEQ, HEAD), P(None, HEAD)),
        check_vma=False,
    )
```

```python
import functools

import jax
import jax.numpy as jnp
from jax import lax
from jax.experimental import pallas as pl
from jax.experimental.pallas import tpu as pltpu
from jax.sharding import Mesh, PartitionSpec as P

HD = 64
WIN = 128
EPSILON = 1e-05
HIGHEST = lax.Precision.HIGHEST
SEQ = ("zh", "y", "core")
HEAD = ("x", "zl")
F32 = jnp.float32
BF16 = jnp.bfloat16
PAD = 48


def shifted(value, by):
    count = lax.axis_size(SEQ)
    pairs = [(i, i + by) for i in range(count) if 0 <= i + by < count]
    return lax.ppermute(value, SEQ, pairs)


def gathered(value, axes):
    count = lax.axis_size(axes)
    spread = jnp.broadcast_to(value[None], (count,) + value.shape)
    return lax.all_to_all(spread, axes, 0, 0)


def dot(left, right, dims, **kw):
    return lax.dot_general(left, right, (dims, ((), ())), preferred_element_type=F32, **kw)


def blocked(rows):
    width = rows.shape[-1]
    parts = rows.reshape(4, 8, 2, -1, width).transpose(1, 2, 0, 3, 4)
    parts = jnp.pad(parts, ((0, 0), (0, 0), (0, 0), (0, PAD - parts.shape[3]), (0, 0)))
    return parts.reshape(-1, width)


def unpadded(rows, row_count):
    width = rows.shape[-1]
    return rows.reshape(8, PAD, width)[:, : row_count // 8].reshape(row_count, width)


def split3(value):
    high = lax.reduce_precision(value, 8, 7)
    rest = value - high
    mid = lax.reduce_precision(rest, 8, 7)
    return jnp.stack([high, mid, lax.reduce_precision(rest - mid, 8, 7)])


def mm(left, right, left_dim, right_dim):
    dims = (((left_dim,), (right_dim,)), ((), ()))
    return lax.dot_general(left, right, dims, preferred_element_type=F32)


def pack_kernel(w_query, w_out, w_key, w_value, out):
    rows = w_query.shape[0]
    width = w_query.shape[1]
    out[...] = jnp.zeros(out.shape, BF16)
    for place in range(out.shape[0]):
        out[place, :rows, :width] = w_query[...]
        out[place, :rows, width : 2 * width] = w_out[...]
        out[place, :rows, 2 * width : 2 * width + HD] = w_key[...]
        out[place, :rows, 2 * width + HD :] = w_value[...]


CHUNK = 8 * PAD


def scatter_rows(blocks, row, term):
    for piece in range(CHUNK // PAD):
        number = row // PAD + piece
        z, line = number % 4, number // 4
        place = line % 8 * PAD
        group = z * 2 + line // 8
        blocks[group, place : place + PAD, :] = term[piece * PAD : (piece + 1) * PAD]


def send_blocks(blocks, blocks_hbm, sems, groups):
    sent = []
    for group in groups:
        copy = pltpu.make_async_copy(blocks.at[group], blocks_hbm.at[group], sems.at[group])
        copy.start()
        sent.append(copy)
    return sent


def attend_kernel(
    w_hbm, x_hbm, g_hbm, kv, halo, mask, blocks_hbm, grad_query, grad_halo, grad_kv, *scratch
):
    weight, normed, grads, blocks, sems, out_sems = scratch
    rows_all = weight.shape[0]
    width = weight.shape[1] // 2
    two = 2 * HD
    x_copy = pltpu.make_async_copy(x_hbm, normed, sems.at[0])
    g_copy = pltpu.make_async_copy(g_hbm, grads, sems.at[1])

    def fetch(column, sem):
        part = pl.ds(column, two)
        return pltpu.make_async_copy(w_hbm.at[:, part], weight.at[:, part], sems.at[sem])

    q_copies = [fetch(two * pair, 2 + 2 * pair) for pair in range(4)]
    o_copies = [fetch(width + two * pair, 3 + 2 * pair) for pair in range(4)]
    x_copy.start()
    q_copies[0].start()
    g_copy.start()
    o_copies[0].start()
    for pair in range(1, 4):
        q_copies[pair].start()
        o_copies[pair].start()
    keys = jnp.concatenate([halo[:HD, :], kv[:HD, :]], axis=1)
    values = jnp.concatenate([halo[HD:, :], kv[HD:, :]], axis=1)
    allowed = mask[...] > 0.0
    late = lax.broadcasted_iota(jnp.int32, (WIN, WIN), 0) > lax.broadcasted_iota(
        jnp.int32, (WIN, WIN), 1
    )

    def folded(wide):
        return jnp.where(late, wide[:WIN], wide[WIN:])

    def unfolded(value):
        zero = jnp.zeros_like(value)
        parts = [jnp.where(late, value, zero), jnp.where(late, zero, value)]
        return jnp.concatenate(parts, axis=0).astype(BF16)

    grad_keys = grad_values = jnp.zeros((HD, 2 * WIN), F32)
    mixed = []
    for head in range(8):
        pair = head // 2
        if head % 2 == 0:
            if head == 0:
                x_copy.wait()
            q_copies[pair].wait()
            columns = slice(two * pair, two * (pair + 1))
            query_two = mm(weight[:, columns], normed[...], 0, 0).astype(BF16)
            if head == 0:
                g_copy.wait()
            o_copies[pair].wait()
            columns = slice(width + two * pair, width + two * (pair + 1))
            grad_two = mm(weight[:, columns], grads[...], 0, 0).astype(BF16)
        rows = slice(head % 2 * HD, (head % 2 + 1) * HD)
        query, grad = query_two[rows], grad_two[rows]
        scores = folded(mm(keys, query, 0, 0)) * HD**-0.5
        scores = jnp.where(allowed, scores, -jnp.inf)
        raised = jnp.exp(scores - jnp.max(scores, axis=0, keepdims=True))
        prob = raised * (1.0 / jnp.sum(raised, axis=0, keepdims=True))
        prob_b = unfolded(prob)
        mixed.append(mm(values, prob_b, 1, 0).astype(BF16))
        grad_values += mm(grad, prob_b, 1, 1)
        grad_prob = folded(mm(values, grad, 0, 0))
        delta = jnp.sum(prob * grad_prob, axis=0, keepdims=True)
        grad_scores = unfolded(prob * (grad_prob - delta) * HD**-0.5)
        rows = slice(head * HD, (head + 1) * HD)
        grad_query[rows, :] = mm(keys, grad_scores, 1, 0).astype(BF16)
        grad_keys += mm(query, grad_scores, 1, 1)
    grad_halo[:HD, :] = grad_keys[:, :WIN].astype(BF16)
    grad_halo[HD:, :] = grad_values[:, :WIN].astype(BF16)
    grad_kv[:HD, :] = grad_keys[:, WIN:]
    grad_kv[HD:, :] = grad_values[:, WIN:]
    mixed = jnp.concatenate(mixed, axis=0)
    sent = []
    for row in range(0, rows_all, CHUNK):
        term = mm(weight[row : row + CHUNK, width:], mixed, 1, 0).astype(BF16)
        scatter_rows(blocks, row, term)
        if row + CHUNK == rows_all // 2:
            sent += send_blocks(blocks, blocks_hbm, out_sems, range(0, 8, 2))
    sent += send_blocks(blocks, blocks_hbm, out_sems, range(1, 8, 2))
    for copy in sent:
        copy.wait()


def back_kernel(w_hbm, kv_hbm, x_hbm, grad_query, grad_kv, returned, blocks_hbm, *scratch):
    weight, kv_all, normed, blocks, sems, out_sems = scratch
    width = weight.shape[1]
    rows_all = weight.shape[0]
    size = 2 * CHUNK
    copies = []
    for step in range(rows_all // size):
        rows = pl.ds(step * size, size)
        trio = (
            (w_hbm.at[rows, pl.ds(0, width)], weight.at[rows, :]),
            (kv_hbm.at[rows, :], kv_all.at[rows, :]),
            (x_hbm.at[rows, :], normed.at[rows, :]),
        )
        copies.append(
            [pltpu.make_async_copy(a, b, sems.at[step, k]) for k, (a, b) in enumerate(trio)]
        )
        for copy in copies[-1]:
            copy.start()
    tokens_here = grad_kv.shape[1]
    kv_grad = (grad_kv[...] + returned[...].astype(F32)).astype(BF16)
    grads = grad_query[...]
    total = jnp.zeros((1, tokens_here), F32)
    for row in range(0, rows_all, CHUNK):
        if row % size == 0:
            for copy in copies[row // size]:
                copy.wait()
        rows = slice(row, row + CHUNK)
        term = mm(weight[rows, :], grads, 1, 0) + mm(kv_all[rows, :], kv_grad, 1, 0)
        term = term.astype(BF16)
        scatter_rows(blocks, row, term)
        products = term.astype(F32) * normed[rows, :].astype(F32)
        total = total + jnp.sum(products, axis=0, keepdims=True)
    high = total.astype(BF16).astype(F32)
    mid = (total - high).astype(BF16).astype(F32)
    low = total - high - mid
    line = lax.broadcasted_iota(jnp.int32, (16, tokens_here), 0)
    extra = jnp.where(line == 0, high, jnp.where(line == 1, mid, jnp.where(line == 2, low, 0.0)))
    for group in range(8):
        blocks[group, 8 * PAD :, :] = extra.astype(BF16)
    for copy in send_blocks(blocks, blocks_hbm, out_sems, range(8)):
        copy.wait()


ANY = pl.BlockSpec(memory_space=pltpu.MemorySpace.HBM)
FULL = pl.BlockSpec(memory_space=pltpu.MemorySpace.VMEM)


def call(kernel, outs, in_specs, out_specs, scratch, *args):
    size = sum(a.size * a.dtype.itemsize for a in jax.tree.leaves((args, outs)))
    return pl.pallas_call(
        kernel,
        out_shape=outs,
        in_specs=in_specs,
        out_specs=out_specs,
        scratch_shapes=scratch,
        compiler_params=pltpu.CompilerParams(vmem_limit_bytes=58 * 2**20),
        cost_estimate=pl.CostEstimate(flops=10**8, bytes_accessed=size, transcendentals=0),
    )(*args)


def shards(
    tokens,
    gain,
    w_query,
    w_key,
    w_value,
    w_out,
    w_gate,
    steering,
    segment_ids,
    steer_index,
    grad_out,
):
    row_count, model_width = tokens.shape
    share = model_width // 8
    start = lax.axis_index(HEAD) * share

    width = w_query.shape[1]
    like = jax.ShapeDtypeStruct
    sent = call(
        pack_kernel,
        like((4, PAD, 2 * width + 2 * HD), BF16),
        [FULL] * 4,
        FULL,
        [],
        *(w_query, w_out, w_key, w_value),
    )
    near = lax.all_to_all(sent, "zh", 0, 0)
    whole = lax.all_gather(near[:, :, : 2 * width], ("y", "core"), axis=0, tiled=True)
    whole = whole.reshape(-1, 2 * width)
    kv_near = near[:, :, 2 * width :].reshape(-1, 2 * HD)

    tok = tokens.T.astype(F32)
    inverse = lax.rsqrt(jnp.mean(tok * tok, axis=0, keepdims=True) + EPSILON)
    unit = tok * inverse
    normed = (unit * gain[:, None]).astype(BF16)
    normed_b = blocked(normed)
    grad_t = grad_out.T
    grad_b = blocked(grad_t)
    gate = jax.nn.sigmoid(jnp.sum(normed.astype(F32) * w_gate[:, None], axis=0))
    one_hot = steer_index[None, :] == lax.broadcasted_iota(jnp.int32, (16, row_count), 0)
    products = dot(steering, grad_t, ((1,), (0,)))
    grad_logit = gate * (1.0 - gate) * jnp.sum(jnp.where(one_hot, products, 0.0), axis=0)
    steer_share = lax.dynamic_slice_in_dim(steering, start, share, 1)
    steer_rows = dot(steer_share, one_hot.astype(BF16), ((0,), (0,)))
    grad_share = lax.dynamic_slice_in_dim(grad_t, start, share, 0).astype(F32)
    steer_part = dot(
        one_hot.astype(F32), gate[None, :] * grad_share, ((1,), (1,)), precision=HIGHEST
    )

    steer = jnp.sum(gathered(steer_part, ("zh", "core")), axis=0)
    lanes = 3 * 128
    parts = jnp.pad(split3(steer), ((0, 0), (0, 0), (0, lanes - share))).astype(BF16)
    parts = parts.reshape(-1, lanes)
    parts = [parts[:, k : k + 128] for k in range(0, lanes, 128)]
    kv_rows = kv_near.shape[0]
    both = gathered(jnp.concatenate([kv_near, *parts], axis=0), ("y",))
    kv_all = both[:, :kv_rows].reshape(8, 1, kv_rows, 2 * HD)
    kv_all = lax.all_gather(kv_all, "core", axis=1, tiled=True).reshape(-1, 2 * HD)
    steer = jnp.sum(both[:, kv_rows:].astype(F32), axis=0).reshape(3, 3, 16, 128)
    steer_grad = jnp.sum(steer, axis=1).transpose(1, 0, 2).reshape(16, lanes)[:, :share]

    halo_seg = shifted(segment_ids, 1)
    halo_seg = jnp.where(lax.axis_index(SEQ) > 0, halo_seg, -1)
    kv = dot(kv_all, normed_b, ((0,), (0,))).astype(BF16)
    halo = shifted(kv, 1)
    key_pos = lax.broadcasted_iota(jnp.int32, (row_count, row_count), 0)
    query_pos = lax.broadcasted_iota(jnp.int32, (row_count, row_count), 1)
    key_seg = jnp.where(key_pos > query_pos, halo_seg[:, None], segment_ids[:, None])
    mask = (key_seg == segment_ids[None, :]).astype(F32)
    whole, halo, mask, steer_grad, normed_b, grad_b, kv, kv_all = lax.optimization_barrier(
        (whole, halo, mask, steer_grad, normed_b, grad_b, kv, kv_all)
    )
    total_rows = whole.shape[0]
    dma = pltpu.SemaphoreType.DMA
    blocks, grad_query, grad_halo, grad_kv = call(
        attend_kernel,
        (
            like((8, 8 * PAD, row_count), BF16),
            like((width, row_count), BF16),
            like((2 * HD, row_count), BF16),
            like((2 * HD, row_count), F32),
        ),
        [ANY, ANY, ANY, FULL, FULL, FULL],
        [ANY, FULL, FULL, FULL],
        [
            pltpu.VMEM((total_rows, 2 * width), BF16),
            pltpu.VMEM((total_rows, row_count), BF16),
            pltpu.VMEM((total_rows, row_count), BF16),
            pltpu.VMEM((8, 8 * PAD, row_count), BF16),
            dma((10,)),
            dma((8,)),
        ],
        *(whole, normed_b, grad_b, kv, halo, mask),
    )
    returned = shifted(grad_halo, -1)
    attn = lax.all_to_all(blocks, HEAD, 0, 0)
    back = call(
        back_kernel,
        like((8, 8 * PAD + 16, row_count), BF16),
        [ANY, ANY, ANY, FULL, FULL, FULL],
        ANY,
        [
            pltpu.VMEM((total_rows, width), BF16),
            pltpu.VMEM((total_rows, 2 * HD), BF16),
            pltpu.VMEM((total_rows, row_count), BF16),
            pltpu.VMEM((8, 8 * PAD + 16, row_count), BF16),
            dma((4, 3)),
            dma((8,)),
        ],
        *(whole, kv_all, normed_b, grad_query, grad_kv, returned),
    )
    back = lax.all_to_all(back, HEAD, 0, 0)

    attn_share = unpadded(jnp.sum(attn.astype(F32), axis=0), share)
    token_share = lax.dynamic_slice_in_dim(tokens.T, start, share, 0).astype(F32)
    layer_out = (token_share + attn_share + gate[None, :] * steer_rows).astype(BF16)
    back = jnp.sum(back.astype(F32), axis=0)
    gain_share = lax.dynamic_slice_in_dim(gain, start, share, 0)[:, None]
    gate_share = lax.dynamic_slice_in_dim(w_gate, start, share, 0)[:, None]
    total = unpadded(back[: 8 * PAD], share) + grad_logit[None, :] * gate_share
    gate_total = jnp.sum(unit * (gain * w_gate)[:, None], axis=0)
    row_total = jnp.sum(back[8 * PAD : 8 * PAD + 3], axis=0) + grad_logit * gate_total
    unit_share = token_share * inverse
    scaled = total * gain_share
    grad_tokens = (
        grad_share + inverse * (scaled - unit_share * (row_total / model_width)[None, :])
    ).astype(BF16)
    return (layer_out.T, grad_tokens.T, steer_grad)


def solution(mesh):
    split = Mesh(mesh.devices.reshape(4, 8, 2, 4, 2), SEQ + HEAD)
    placed = (
        P(SEQ, None),
        P(),
        P(SEQ, HEAD),
        P(SEQ, HEAD),
        P(SEQ, HEAD),
        P(SEQ, HEAD),
        P(),
        P(),
        P(SEQ),
        P(SEQ),
        P(SEQ, None),
    )
    return jax.shard_map(
        shards,
        mesh=split,
        in_specs=placed,
        out_specs=(P(SEQ, HEAD), P(SEQ, HEAD), P(None, HEAD)),
        check_vma=False,
    )
```

```python
import functools

import jax
import jax.numpy as jnp
from jax import lax
from jax.experimental import pallas as pl
from jax.experimental.pallas import tpu as pltpu
from jax.sharding import Mesh, PartitionSpec as P

HD = 64
WIN = 128
EPSILON = 1e-05
HIGHEST = lax.Precision.HIGHEST
SEQ = ("zh", "y", "core")
HEAD = ("x", "zl")
F32 = jnp.float32
BF16 = jnp.bfloat16
PAD = 48


def shifted(value, by):
    count = lax.axis_size(SEQ)
    pairs = [(i, i + by) for i in range(count) if 0 <= i + by < count]
    return lax.ppermute(value, SEQ, pairs)


def gathered(value, axes):
    count = lax.axis_size(axes)
    spread = jnp.broadcast_to(value[None], (count,) + value.shape)
    return lax.all_to_all(spread, axes, 0, 0)


def dot(left, right, dims, **kw):
    return lax.dot_general(left, right, (dims, ((), ())), preferred_element_type=F32, **kw)


def blocked(rows):
    width = rows.shape[-1]
    parts = rows.reshape(4, 8, 2, -1, width).transpose(1, 2, 0, 3, 4)
    parts = jnp.pad(parts, ((0, 0), (0, 0), (0, 0), (0, PAD - parts.shape[3]), (0, 0)))
    return parts.reshape(-1, width)


def unpadded(rows, row_count):
    width = rows.shape[-1]
    return rows.reshape(8, PAD, width)[:, : row_count // 8].reshape(row_count, width)


def mm(left, right, left_dim, right_dim):
    dims = (((left_dim,), (right_dim,)), ((), ()))
    return lax.dot_general(left, right, dims, preferred_element_type=F32)


def pack_kernel(q_hbm, o_hbm, k_hbm, v_hbm, out_hbm, query, out, key, value, packed, sems):
    pairs = ((q_hbm, query), (o_hbm, out), (k_hbm, key), (v_hbm, value))
    copies = start_all(pairs, sems)
    rows, width = query.shape
    packed[rows // 8 * 8 :, :] = jnp.zeros((PAD - rows // 8 * 8, packed.shape[1]), BF16)
    for copy in copies:
        copy.wait()
    packed[:rows, :width] = query[...]
    packed[:rows, width : 2 * width] = out[...]
    packed[:rows, 2 * width :] = jnp.concatenate([key[...], value[...]], axis=1)
    places = [(packed, out_hbm.at[place]) for place in range(out_hbm.shape[0])]
    for copy in start_all(places, sems):
        copy.wait()


CHUNK = 8 * PAD


def scatter_rows(blocks, row, term):
    for piece in range(CHUNK // PAD):
        number = row // PAD + piece
        z, line = number % 4, number // 4
        place = line % 8 * PAD
        group = z * 2 + line // 8
        blocks[group, place : place + PAD, :] = term[piece * PAD : (piece + 1) * PAD]


def send_blocks(blocks, blocks_hbm, sems, groups):
    sent = []
    for group in groups:
        copy = pltpu.make_async_copy(blocks.at[group], blocks_hbm.at[group], sems.at[group])
        copy.start()
        sent.append(copy)
    return sent


def start_all(pairs, sems):
    copies = [pltpu.make_async_copy(a, b, sems.at[k]) for k, (a, b) in enumerate(pairs)]
    for copy in copies:
        copy.start()
    return copies


def attend_kernel(
    w_hbm, x_hbm, g_hbm, kv_hbm, halo_hbm, mask_hbm, blocks_hbm, dq_hbm, dh_hbm, dkv_hbm, *scratch
):
    weight, normed, grads, kv, halo, mask, blocks, grad_query, grad_halo, grad_kv = scratch[:10]
    sems, out_sems = scratch[10:]
    rows_all = weight.shape[0]
    width = weight.shape[1] // 2
    together = 4
    span = together * HD
    pairs = [(x_hbm, normed)]
    for column in range(0, width, span):
        for first in (column, width + column):
            part = pl.ds(first, span)
            pairs.append((w_hbm.at[:, part], weight.at[:, part]))
        if column == 0:
            pairs.insert(2, (g_hbm, grads))
            pairs += [(kv_hbm, kv), (halo_hbm, halo), (mask_hbm, mask)]
    copies = start_all(pairs, sems)
    late = lax.broadcasted_iota(jnp.int32, (WIN, WIN), 0) > lax.broadcasted_iota(
        jnp.int32, (WIN, WIN), 1
    )
    late = jnp.concatenate([late] * together, axis=1)

    def folded(wide):
        return jnp.where(late, wide[:WIN], wide[WIN:])

    def unfolded(value):
        zero = jnp.zeros_like(value)
        parts = [jnp.where(late, value, zero), jnp.where(late, zero, value)]
        return jnp.concatenate(parts, axis=0).astype(BF16)

    def beside(rows):
        return jnp.concatenate([rows[k : k + HD] for k in range(0, span, HD)], axis=1)

    def stacked(lanes):
        return jnp.concatenate([lanes[:, k * WIN : (k + 1) * WIN] for k in range(together)], axis=0)

    grad_keys = grad_values = jnp.zeros((HD, 2 * WIN), F32)
    mixed = []
    for column in range(0, width, span):
        if column == 0:
            for copy in copies[:2]:
                copy.wait()
        else:
            copies[5 + 2 * column // span].wait()
        query = mm(weight[:, column : column + span], normed[...], 0, 0).astype(BF16)
        if column == 0:
            for copy in copies[2:7]:
                copy.wait()
            keys = jnp.concatenate([halo[:HD, :], kv[:HD, :]], axis=1)
            values = jnp.concatenate([halo[HD:, :], kv[HD:, :]], axis=1)
            allowed = jnp.concatenate([mask[...] > 0.0] * together, axis=1)
        else:
            copies[6 + 2 * column // span].wait()
        first = width + column
        grad = mm(weight[:, first : first + span], grads[...], 0, 0).astype(BF16)
        query, grad = beside(query), beside(grad)
        scores = folded(mm(keys, query, 0, 0)) * HD**-0.5
        scores = jnp.where(allowed, scores, -jnp.inf)
        raised = jnp.exp(scores - jnp.max(scores, axis=0, keepdims=True))
        prob = raised * (1.0 / jnp.sum(raised, axis=0, keepdims=True))
        prob_b = unfolded(prob)
        mixed.append(stacked(mm(values, prob_b, 1, 0).astype(BF16)))
        grad_values += mm(grad, prob_b, 1, 1)
        grad_prob = folded(mm(values, grad, 0, 0))
        delta = jnp.sum(prob * grad_prob, axis=0, keepdims=True)
        grad_scores = unfolded(prob * (grad_prob - delta) * HD**-0.5)
        grad_query[column : column + span, :] = stacked(mm(keys, grad_scores, 1, 0).astype(BF16))
        grad_keys += mm(query, grad_scores, 1, 1)
    grad_halo[:HD, :] = grad_keys[:, :WIN].astype(BF16)
    grad_halo[HD:, :] = grad_values[:, :WIN].astype(BF16)
    grad_kv[:HD, :] = grad_keys[:, WIN:]
    grad_kv[HD:, :] = grad_values[:, WIN:]
    results = ((grad_query, dq_hbm), (grad_halo, dh_hbm), (grad_kv, dkv_hbm))
    sent = start_all(results, out_sems.at[pl.ds(8, 3)])
    mixed = jnp.concatenate(mixed, axis=0)
    for row in range(0, rows_all, CHUNK):
        term = mm(weight[row : row + CHUNK, width:], mixed, 1, 0).astype(BF16)
        scatter_rows(blocks, row, term)
        if row + CHUNK == rows_all // 2:
            sent += send_blocks(blocks, blocks_hbm, out_sems, range(0, 8, 2))
    sent += send_blocks(blocks, blocks_hbm, out_sems, range(1, 8, 2))
    for copy in sent:
        copy.wait()


def back_kernel(w_hbm, kv_hbm, x_hbm, dq_hbm, dkv_hbm, ret_hbm, blocks_hbm, *scratch):
    weight, kv_all, normed, grad_query, grad_kv, returned, blocks, sems, out_sems = scratch
    results = ((dq_hbm, grad_query), (dkv_hbm, grad_kv), (ret_hbm, returned))
    small = start_all(results, sems.at[weight.shape[0] // (2 * CHUNK)])
    width = weight.shape[1]
    rows_all = weight.shape[0]
    size = 2 * CHUNK
    copies = []
    for step in range(rows_all // size):
        rows = pl.ds(step * size, size)
        trio = (
            (w_hbm.at[rows, pl.ds(0, width)], weight.at[rows, :]),
            (kv_hbm.at[rows, :], kv_all.at[rows, :]),
            (x_hbm.at[rows, :], normed.at[rows, :]),
        )
        copies.append(
            [pltpu.make_async_copy(a, b, sems.at[step, k]) for k, (a, b) in enumerate(trio)]
        )
        for copy in copies[-1]:
            copy.start()
    for copy in small:
        copy.wait()
    tokens_here = grad_kv.shape[1]
    kv_grad = (grad_kv[...] + returned[...].astype(F32)).astype(BF16)
    grads = grad_query[...]
    total = jnp.zeros((1, tokens_here), F32)
    for row in range(0, rows_all, CHUNK):
        if row % size == 0:
            for copy in copies[row // size]:
                copy.wait()
        rows = slice(row, row + CHUNK)
        term = mm(weight[rows, :], grads, 1, 0) + mm(kv_all[rows, :], kv_grad, 1, 0)
        term = term.astype(BF16)
        scatter_rows(blocks, row, term)
        products = term.astype(F32) * normed[rows, :].astype(F32)
        total = total + jnp.sum(products, axis=0, keepdims=True)
    high = total.astype(BF16).astype(F32)
    mid = (total - high).astype(BF16).astype(F32)
    low = total - high - mid
    line = lax.broadcasted_iota(jnp.int32, (8, tokens_here), 0)
    extra = jnp.where(line == 0, high, jnp.where(line == 1, mid, jnp.where(line == 2, low, 0.0)))
    for group in range(8):
        blocks[group, 8 * PAD :, :] = extra.astype(BF16)
    for copy in send_blocks(blocks, blocks_hbm, out_sems, range(8)):
        copy.wait()


HBM = pl.BlockSpec(memory_space=pltpu.MemorySpace.HBM)
ANY = pl.BlockSpec(memory_space=pl.ANY)


def call(kernel, outs, in_specs, out_specs, scratch, *args):
    size = sum(a.size * a.dtype.itemsize for a in jax.tree.leaves((args, outs)))
    return pl.pallas_call(
        kernel,
        out_shape=outs,
        in_specs=in_specs,
        out_specs=out_specs,
        scratch_shapes=scratch,
        compiler_params=pltpu.CompilerParams(vmem_limit_bytes=58 * 2**20),
        cost_estimate=pl.CostEstimate(flops=10**8, bytes_accessed=size, transcendentals=0),
    )(*args)


def shards(
    tokens,
    gain,
    w_query,
    w_key,
    w_value,
    w_out,
    w_gate,
    steering,
    segment_ids,
    steer_index,
    grad_out,
):
    row_count, model_width = tokens.shape
    share = model_width // 8
    start = lax.axis_index(HEAD) * share

    width = w_query.shape[1]
    like = jax.ShapeDtypeStruct
    sent = call(
        pack_kernel,
        like((4, PAD, 2 * width + 2 * HD), BF16),
        [ANY] * 4,
        HBM,
        [
            *[pltpu.VMEM(w.shape, BF16) for w in (w_query, w_out, w_key, w_value)],
            pltpu.VMEM((PAD, 2 * width + 2 * HD), BF16),
            pltpu.SemaphoreType.DMA((4,)),
        ],
        *(w_query, w_out, w_key, w_value),
    )
    near = lax.all_to_all(sent, "zh", 0, 0)
    whole = lax.all_gather(near[:, :, : 2 * width], ("y", "core"), axis=0, tiled=True)
    whole = whole.reshape(-1, 2 * width)
    kv_near = gathered(near[:, :, 2 * width :], ("y",))
    kv_all = lax.all_gather(kv_near[:, None], "core", axis=1, tiled=True).reshape(-1, 2 * HD)

    tok = tokens.T.astype(F32)
    inverse = lax.rsqrt(jnp.mean(tok * tok, axis=0, keepdims=True) + EPSILON)
    unit = tok * inverse
    normed = (unit * gain[:, None]).astype(BF16)
    normed_b = blocked(normed)
    grad_t = grad_out.T
    grad_b = blocked(grad_t)
    gate = jax.nn.sigmoid(jnp.sum(normed.astype(F32) * w_gate[:, None], axis=0))
    one_hot = steer_index[None, :] == lax.broadcasted_iota(jnp.int32, (16, row_count), 0)
    products = dot(steering, grad_t, ((1,), (0,)))
    grad_logit = gate * (1.0 - gate) * jnp.sum(jnp.where(one_hot, products, 0.0), axis=0)
    steer_share = lax.dynamic_slice_in_dim(steering, start, share, 1)
    steer_rows = dot(steer_share, one_hot.astype(BF16), ((0,), (0,)))
    grad_share = lax.dynamic_slice_in_dim(grad_t, start, share, 0).astype(F32)
    steer_part = dot(
        one_hot.astype(F32), gate[None, :] * grad_share, ((1,), (1,)), precision=HIGHEST
    )


    def exchanged(value, *steps):
        for axis, step in steps:
            pairs = [(i, i ^ step) for i in range(lax.axis_size(axis))]
            value = value + lax.ppermute(value, axis, pairs)
        return value

    steer = exchanged(steer_part, ("core", 1), ("zh", 1))

    halo_seg = shifted(segment_ids, 1)
    halo_seg = jnp.where(lax.axis_index(SEQ) > 0, halo_seg, -1)
    kv = dot(kv_all, normed_b, ((0,), (0,))).astype(BF16)
    halo = shifted(kv, 1)
    key_pos = lax.broadcasted_iota(jnp.int32, (row_count, row_count), 0)
    query_pos = lax.broadcasted_iota(jnp.int32, (row_count, row_count), 1)
    key_seg = jnp.where(key_pos > query_pos, halo_seg[:, None], segment_ids[:, None])
    mask = (key_seg == segment_ids[None, :]).astype(F32)
    steer, halo, kv, mask = lax.optimization_barrier((steer, halo, kv, mask))
    steer = exchanged(steer, ("zh", 2), ("y", 1))
    whole, halo, mask, steer, normed_b, grad_b, kv, kv_all = lax.optimization_barrier(
        (whole, halo, mask, steer, normed_b, grad_b, kv, kv_all)
    )
    total_rows = whole.shape[0]
    dma = pltpu.SemaphoreType.DMA
    blocks, grad_query, grad_halo, grad_kv = call(
        attend_kernel,
        (
            like((8, 8 * PAD, row_count), BF16),
            like((width, row_count), BF16),
            like((2 * HD, row_count), BF16),
            like((2 * HD, row_count), F32),
        ),
        [HBM] * 3 + [ANY] * 3,
        [HBM] + [ANY] * 3,
        [
            pltpu.VMEM((total_rows, 2 * width), BF16),
            pltpu.VMEM((total_rows, row_count), BF16),
            pltpu.VMEM((total_rows, row_count), BF16),
            pltpu.VMEM((2 * HD, row_count), BF16),
            pltpu.VMEM((2 * HD, row_count), BF16),
            pltpu.VMEM((row_count, row_count), F32),
            pltpu.VMEM((8, 8 * PAD, row_count), BF16),
            pltpu.VMEM((width, row_count), BF16),
            pltpu.VMEM((2 * HD, row_count), BF16),
            pltpu.VMEM((2 * HD, row_count), F32),
            dma((9,)),
            dma((11,)),
        ],
        *(whole, normed_b, grad_b, kv, halo, mask),
    )
    returned = shifted(grad_halo, -1)
    attn = lax.all_to_all(blocks, HEAD, 0, 0)
    steer, grad_kv = lax.optimization_barrier((steer, grad_kv))
    steer = exchanged(steer, ("y", 2))
    steer, returned, grad_kv = lax.optimization_barrier((steer, returned, grad_kv))
    back = call(
        back_kernel,
        like((8, 8 * PAD + 8, row_count), BF16),
        [HBM] * 3 + [ANY] * 3,
        HBM,
        [
            pltpu.VMEM((total_rows, width), BF16),
            pltpu.VMEM((total_rows, 2 * HD), BF16),
            pltpu.VMEM((total_rows, row_count), BF16),
            pltpu.VMEM((width, row_count), BF16),
            pltpu.VMEM((2 * HD, row_count), F32),
            pltpu.VMEM((2 * HD, row_count), BF16),
            pltpu.VMEM((8, 8 * PAD + 8, row_count), BF16),
            dma((5, 3)),
            dma((8,)),
        ],
        *(whole, kv_all, normed_b, grad_query, grad_kv, returned),
    )
    steer, back = lax.optimization_barrier((steer, back))
    back = lax.all_to_all(back, HEAD, 0, 0)
    steer_grad = exchanged(steer, ("y", 4))

    attn_share = unpadded(jnp.sum(attn.astype(F32), axis=0), share)
    token_share = lax.dynamic_slice_in_dim(tokens.T, start, share, 0).astype(F32)
    layer_out = (token_share + attn_share + gate[None, :] * steer_rows).astype(BF16)
    back = jnp.sum(back.astype(F32), axis=0)
    gain_share = lax.dynamic_slice_in_dim(gain, start, share, 0)[:, None]
    gate_share = lax.dynamic_slice_in_dim(w_gate, start, share, 0)[:, None]
    total = unpadded(back[: 8 * PAD], share) + grad_logit[None, :] * gate_share
    gate_total = jnp.sum(unit * (gain * w_gate)[:, None], axis=0)
    row_total = jnp.sum(back[8 * PAD : 8 * PAD + 3], axis=0) + grad_logit * gate_total
    unit_share = token_share * inverse
    scaled = total * gain_share
    grad_tokens = (
        grad_share + inverse * (scaled - unit_share * (row_total / model_width)[None, :])
    ).astype(BF16)
    return (layer_out.T, grad_tokens.T, steer_grad)


def solution(mesh):
    split = Mesh(mesh.devices.reshape(4, 8, 2, 4, 2), SEQ + HEAD)
    placed = (
        P(SEQ, None),
        P(),
        P(SEQ, HEAD),
        P(SEQ, HEAD),
        P(SEQ, HEAD),
        P(SEQ, HEAD),
        P(),
        P(),
        P(SEQ),
        P(SEQ),
        P(SEQ, None),
    )
    return jax.shard_map(
        shards,
        mesh=split,
        in_specs=placed,
        out_specs=(P(SEQ, HEAD), P(SEQ, HEAD), P(None, HEAD)),
        check_vma=False,
    )
```

```python
import functools

import jax
import jax.numpy as jnp
from jax import lax
from jax.experimental import pallas as pl
from jax.experimental.pallas import tpu as pltpu
from jax.sharding import Mesh, PartitionSpec as P

HD = 64
WIN = 128
EPSILON = 1e-05
HIGHEST = lax.Precision.HIGHEST
SEQ = ("zh", "y", "core")
HEAD = ("x", "zl")
F32 = jnp.float32
BF16 = jnp.bfloat16
PAD = 48


def shifted(value, by):
    count = lax.axis_size(SEQ)
    pairs = [(i, i + by) for i in range(count) if 0 <= i + by < count]
    return lax.ppermute(value, SEQ, pairs)


def gathered(value, axes):
    count = lax.axis_size(axes)
    spread = jnp.broadcast_to(value[None], (count,) + value.shape)
    return lax.all_to_all(spread, axes, 0, 0)


def dot(left, right, dims, **kw):
    return lax.dot_general(left, right, (dims, ((), ())), preferred_element_type=F32, **kw)


def blocked(rows):
    width = rows.shape[-1]
    parts = rows.reshape(4, 8, 2, -1, width).transpose(1, 2, 0, 3, 4)
    parts = jnp.pad(parts, ((0, 0), (0, 0), (0, 0), (0, PAD - parts.shape[3]), (0, 0)))
    return parts.reshape(-1, width)


def unpadded(rows, row_count):
    width = rows.shape[-1]
    return rows.reshape(8, PAD, width)[:, : row_count // 8].reshape(row_count, width)


def mm(left, right, left_dim, right_dim):
    dims = (((left_dim,), (right_dim,)), ((), ()))
    return lax.dot_general(left, right, dims, preferred_element_type=F32)


def pack_kernel(q_hbm, o_hbm, k_hbm, v_hbm, out_hbm, query, out, key, value, packed, sems):
    pairs = ((q_hbm, query), (o_hbm, out), (k_hbm, key), (v_hbm, value))
    copies = start_all(pairs, sems)
    rows, width = query.shape
    packed[rows // 8 * 8 :, :] = jnp.zeros((PAD - rows // 8 * 8, packed.shape[1]), BF16)
    for copy in copies:
        copy.wait()
    packed[:rows, :width] = query[...]
    packed[:rows, width : 2 * width] = out[...]
    packed[:rows, 2 * width :] = jnp.concatenate([key[...], value[...]], axis=1)
    places = [(packed, out_hbm.at[place]) for place in range(out_hbm.shape[0])]
    for copy in start_all(places, sems):
        copy.wait()


CHUNK = 8 * PAD


def scatter_rows(blocks, row, term):
    for piece in range(CHUNK // PAD):
        number = row // PAD + piece
        z, line = number % 4, number // 4
        place = line % 8 * PAD
        group = z * 2 + line // 8
        blocks[group, place : place + PAD, :] = term[piece * PAD : (piece + 1) * PAD]


def send_blocks(blocks, blocks_hbm, sems, groups):
    sent = []
    for group in groups:
        copy = pltpu.make_async_copy(blocks.at[group], blocks_hbm.at[group], sems.at[group])
        copy.start()
        sent.append(copy)
    return sent


def start_all(pairs, sems):
    copies = [pltpu.make_async_copy(a, b, sems.at[k]) for k, (a, b) in enumerate(pairs)]
    for copy in copies:
        copy.start()
    return copies


def attend_kernel(
    w_hbm, x_hbm, g_hbm, kv_hbm, halo_hbm, mask_hbm, blocks_hbm, dq_hbm, dh_hbm, dkv_hbm, *scratch
):
    weight, normed, grads, kv, halo, mask, blocks, grad_query, grad_halo, grad_kv = scratch[:10]
    sems, out_sems = scratch[10:]
    rows_all = weight.shape[0]
    width = weight.shape[1] // 2
    together = 4
    span = together * HD
    pairs = [(x_hbm, normed)]
    for column in range(0, width, span):
        for first in (column, width + column):
            part = pl.ds(first, span)
            pairs.append((w_hbm.at[:, part], weight.at[:, part]))
        if column == 0:
            pairs.insert(2, (g_hbm, grads))
            pairs += [(kv_hbm, kv), (halo_hbm, halo), (mask_hbm, mask)]
    copies = start_all(pairs, sems)
    late = lax.broadcasted_iota(jnp.int32, (WIN, WIN), 0) > lax.broadcasted_iota(
        jnp.int32, (WIN, WIN), 1
    )
    late = jnp.concatenate([late] * together, axis=1)

    def folded(wide):
        return jnp.where(late, wide[:WIN], wide[WIN:])

    def unfolded(value):
        zero = jnp.zeros_like(value)
        parts = [jnp.where(late, value, zero), jnp.where(late, zero, value)]
        return jnp.concatenate(parts, axis=0).astype(BF16)

    def beside(rows):
        return jnp.concatenate([rows[k : k + HD] for k in range(0, span, HD)], axis=1)

    def stacked(lanes):
        return jnp.concatenate([lanes[:, k * WIN : (k + 1) * WIN] for k in range(together)], axis=0)

    grad_keys = grad_values = jnp.zeros((HD, 2 * WIN), F32)
    mixed = []
    for column in range(0, width, span):
        if column == 0:
            for copy in copies[:2]:
                copy.wait()
        else:
            copies[5 + 2 * column // span].wait()
        query = mm(weight[:, column : column + span], normed[...], 0, 0).astype(BF16)
        if column == 0:
            for copy in copies[2:7]:
                copy.wait()
            keys = jnp.concatenate([halo[:HD, :], kv[:HD, :]], axis=1)
            values = jnp.concatenate([halo[HD : 2 * HD, :], kv[HD:, :]], axis=1)
            allowed = jnp.concatenate([mask[...] > 0.0] * together, axis=1)
        else:
            copies[6 + 2 * column // span].wait()
        first = width + column
        grad = mm(weight[:, first : first + span], grads[...], 0, 0).astype(BF16)
        query, grad = beside(query), beside(grad)
        scores = folded(mm(keys, query, 0, 0)) * HD**-0.5
        scores = jnp.where(allowed, scores, -jnp.inf)
        raised = jnp.exp(scores - jnp.max(scores, axis=0, keepdims=True))
        prob = raised * (1.0 / jnp.sum(raised, axis=0, keepdims=True))
        prob_b = unfolded(prob)
        mixed.append(stacked(mm(values, prob_b, 1, 0).astype(BF16)))
        grad_values += mm(grad, prob_b, 1, 1)
        grad_prob = folded(mm(values, grad, 0, 0))
        delta = jnp.sum(prob * grad_prob, axis=0, keepdims=True)
        grad_scores = unfolded(prob * (grad_prob - delta) * HD**-0.5)
        grad_query[column : column + span, :] = stacked(mm(keys, grad_scores, 1, 0).astype(BF16))
        grad_keys += mm(query, grad_scores, 1, 1)
    grad_halo[:HD, :] = grad_keys[:, :WIN].astype(BF16)
    grad_halo[HD:, :] = grad_values[:, :WIN].astype(BF16)
    grad_kv[:HD, :] = grad_keys[:, WIN:]
    grad_kv[HD:, :] = grad_values[:, WIN:]
    results = ((grad_query, dq_hbm), (grad_halo, dh_hbm), (grad_kv, dkv_hbm))
    sent = start_all(results, out_sems.at[pl.ds(8, 3)])
    mixed = jnp.concatenate(mixed, axis=0)
    for row in range(0, rows_all, CHUNK):
        term = mm(weight[row : row + CHUNK, width:], mixed, 1, 0).astype(BF16)
        scatter_rows(blocks, row, term)
        if row + CHUNK == rows_all // 2:
            sent += send_blocks(blocks, blocks_hbm, out_sems, range(0, 8, 2))
    sent += send_blocks(blocks, blocks_hbm, out_sems, range(1, 8, 2))
    for copy in sent:
        copy.wait()


def back_kernel(w_hbm, kv_hbm, x_hbm, dq_hbm, dkv_hbm, ret_hbm, blocks_hbm, *scratch):
    weight, kv_all, normed, grad_query, grad_kv, returned, blocks, sems, out_sems = scratch
    results = ((dq_hbm, grad_query), (dkv_hbm, grad_kv), (ret_hbm, returned))
    small = start_all(results, sems.at[weight.shape[0] // (2 * CHUNK)])
    width = weight.shape[1]
    rows_all = weight.shape[0]
    size = 2 * CHUNK
    copies = []
    for step in range(rows_all // size):
        rows = pl.ds(step * size, size)
        trio = (
            (w_hbm.at[rows, pl.ds(0, width)], weight.at[rows, :]),
            (kv_hbm.at[rows, :], kv_all.at[rows, :]),
            (x_hbm.at[rows, :], normed.at[rows, :]),
        )
        copies.append(
            [pltpu.make_async_copy(a, b, sems.at[step, k]) for k, (a, b) in enumerate(trio)]
        )
        for copy in copies[-1]:
            copy.start()
    for copy in small:
        copy.wait()
    tokens_here = grad_kv.shape[1]
    kv_grad = (grad_kv[...] + returned[...].astype(F32)).astype(BF16)
    grads = grad_query[...]
    total = jnp.zeros((1, tokens_here), F32)
    for row in range(0, rows_all, CHUNK):
        if row % size == 0:
            for copy in copies[row // size]:
                copy.wait()
        rows = slice(row, row + CHUNK)
        term = mm(weight[rows, :], grads, 1, 0) + mm(kv_all[rows, :], kv_grad, 1, 0)
        term = term.astype(BF16)
        scatter_rows(blocks, row, term)
        products = term.astype(F32) * normed[rows, :].astype(F32)
        total = total + jnp.sum(products, axis=0, keepdims=True)
    high = total.astype(BF16).astype(F32)
    mid = (total - high).astype(BF16).astype(F32)
    low = total - high - mid
    line = lax.broadcasted_iota(jnp.int32, (8, tokens_here), 0)
    extra = jnp.where(line == 0, high, jnp.where(line == 1, mid, jnp.where(line == 2, low, 0.0)))
    for group in range(8):
        blocks[group, 8 * PAD :, :] = extra.astype(BF16)
    for copy in send_blocks(blocks, blocks_hbm, out_sems, range(8)):
        copy.wait()


HBM = pl.BlockSpec(memory_space=pltpu.MemorySpace.HBM)
ANY = pl.BlockSpec(memory_space=pl.ANY)


def call(kernel, outs, in_specs, out_specs, scratch, *args):
    size = sum(a.size * a.dtype.itemsize for a in jax.tree.leaves((args, outs)))
    return pl.pallas_call(
        kernel,
        out_shape=outs,
        in_specs=in_specs,
        out_specs=out_specs,
        scratch_shapes=scratch,
        compiler_params=pltpu.CompilerParams(vmem_limit_bytes=58 * 2**20),
        cost_estimate=pl.CostEstimate(flops=10**8, bytes_accessed=size, transcendentals=0),
    )(*args)


def shards(
    tokens,
    gain,
    w_query,
    w_key,
    w_value,
    w_out,
    w_gate,
    steering,
    segment_ids,
    steer_index,
    grad_out,
):
    row_count, model_width = tokens.shape
    share = model_width // 8
    start = lax.axis_index(HEAD) * share

    width = w_query.shape[1]
    like = jax.ShapeDtypeStruct
    sent = call(
        pack_kernel,
        like((4, PAD, 2 * width + 2 * HD), BF16),
        [ANY] * 4,
        HBM,
        [
            *[pltpu.VMEM(w.shape, BF16) for w in (w_query, w_out, w_key, w_value)],
            pltpu.VMEM((PAD, 2 * width + 2 * HD), BF16),
            pltpu.SemaphoreType.DMA((4,)),
        ],
        *(w_query, w_out, w_key, w_value),
    )
    near = lax.all_to_all(sent, "zh", 0, 0)
    whole = lax.all_gather(near[:, :, : 2 * width], ("y", "core"), axis=0, tiled=True)
    whole = whole.reshape(-1, 2 * width)
    kv_near = gathered(near[:, :, 2 * width :], ("y",))
    kv_all = lax.all_gather(kv_near[:, None], "core", axis=1, tiled=True).reshape(-1, 2 * HD)

    tok = tokens.T.astype(F32)
    inverse = lax.rsqrt(jnp.mean(tok * tok, axis=0, keepdims=True) + EPSILON)
    unit = tok * inverse
    normed = (unit * gain[:, None]).astype(BF16)
    normed_b = blocked(normed)
    grad_t = grad_out.T
    grad_b = blocked(grad_t)
    gate = jax.nn.sigmoid(jnp.sum(normed.astype(F32) * w_gate[:, None], axis=0))
    one_hot = steer_index[None, :] == lax.broadcasted_iota(jnp.int32, (16, row_count), 0)
    products = dot(steering, grad_t, ((1,), (0,)))
    grad_logit = gate * (1.0 - gate) * jnp.sum(jnp.where(one_hot, products, 0.0), axis=0)
    steer_share = lax.dynamic_slice_in_dim(steering, start, share, 1)
    steer_rows = dot(steer_share, one_hot.astype(BF16), ((0,), (0,)))
    grad_share = lax.dynamic_slice_in_dim(grad_t, start, share, 0).astype(F32)
    steer_part = dot(
        one_hot.astype(F32), gate[None, :] * grad_share, ((1,), (1,)), precision=HIGHEST
    )


    def exchanged(value, *steps):
        for axis, step in steps:
            pairs = [(i, i ^ step) for i in range(lax.axis_size(axis))]
            value = value + lax.ppermute(value, axis, pairs)
        return value

    steer = exchanged(steer_part, ("core", 1), ("zh", 1))

    kv = dot(kv_all, normed_b, ((0,), (0,))).astype(BF16)
    ids = jnp.broadcast_to(segment_ids.astype(BF16)[None], (8, row_count))
    halo = shifted(jnp.concatenate([kv, ids], axis=0), 1)
    halo_seg = halo[2 * HD].astype(jnp.int32)
    halo_seg = jnp.where(lax.axis_index(SEQ) > 0, halo_seg, -1)
    key_pos = lax.broadcasted_iota(jnp.int32, (row_count, row_count), 0)
    query_pos = lax.broadcasted_iota(jnp.int32, (row_count, row_count), 1)
    key_seg = jnp.where(key_pos > query_pos, halo_seg[:, None], segment_ids[:, None])
    mask = (key_seg == segment_ids[None, :]).astype(F32)
    steer, halo, kv, mask = lax.optimization_barrier((steer, halo, kv, mask))
    steer = exchanged(steer, ("zh", 2), ("y", 1), ("y", 2))
    whole, halo, mask, steer, normed_b, grad_b, kv, kv_all = lax.optimization_barrier(
        (whole, halo, mask, steer, normed_b, grad_b, kv, kv_all)
    )
    total_rows = whole.shape[0]
    dma = pltpu.SemaphoreType.DMA
    blocks, grad_query, grad_halo, grad_kv = call(
        attend_kernel,
        (
            like((8, 8 * PAD, row_count), BF16),
            like((width, row_count), BF16),
            like((2 * HD, row_count), BF16),
            like((2 * HD, row_count), F32),
        ),
        [HBM] * 3 + [ANY] * 3,
        [HBM] + [ANY] * 3,
        [
            pltpu.VMEM((total_rows, 2 * width), BF16),
            pltpu.VMEM((total_rows, row_count), BF16),
            pltpu.VMEM((total_rows, row_count), BF16),
            pltpu.VMEM((2 * HD, row_count), BF16),
            pltpu.VMEM((2 * HD + 8, row_count), BF16),
            pltpu.VMEM((row_count, row_count), F32),
            pltpu.VMEM((8, 8 * PAD, row_count), BF16),
            pltpu.VMEM((width, row_count), BF16),
            pltpu.VMEM((2 * HD, row_count), BF16),
            pltpu.VMEM((2 * HD, row_count), F32),
            dma((9,)),
            dma((11,)),
        ],
        *(whole, normed_b, grad_b, kv, halo, mask),
    )
    returned = shifted(grad_halo, -1)
    attn = lax.all_to_all(blocks, HEAD, 0, 0)
    back = call(
        back_kernel,
        like((8, 8 * PAD + 8, row_count), BF16),
        [HBM] * 3 + [ANY] * 3,
        HBM,
        [
            pltpu.VMEM((total_rows, width), BF16),
            pltpu.VMEM((total_rows, 2 * HD), BF16),
            pltpu.VMEM((total_rows, row_count), BF16),
            pltpu.VMEM((width, row_count), BF16),
            pltpu.VMEM((2 * HD, row_count), F32),
            pltpu.VMEM((2 * HD, row_count), BF16),
            pltpu.VMEM((8, 8 * PAD + 8, row_count), BF16),
            dma((5, 3)),
            dma((8,)),
        ],
        *(whole, kv_all, normed_b, grad_query, grad_kv, returned),
    )
    steer, back = lax.optimization_barrier((steer, back))
    back = lax.all_to_all(back, HEAD, 0, 0)
    steer_grad = exchanged(steer, ("y", 4))

    attn_share = unpadded(jnp.sum(attn.astype(F32), axis=0), share)
    token_share = lax.dynamic_slice_in_dim(tokens.T, start, share, 0).astype(F32)
    layer_out = (token_share + attn_share + gate[None, :] * steer_rows).astype(BF16)
    back = jnp.sum(back.astype(F32), axis=0)
    gain_share = lax.dynamic_slice_in_dim(gain, start, share, 0)[:, None]
    gate_share = lax.dynamic_slice_in_dim(w_gate, start, share, 0)[:, None]
    total = unpadded(back[: 8 * PAD], share) + grad_logit[None, :] * gate_share
    gate_total = jnp.sum(unit * (gain * w_gate)[:, None], axis=0)
    row_total = jnp.sum(back[8 * PAD : 8 * PAD + 3], axis=0) + grad_logit * gate_total
    unit_share = token_share * inverse
    scaled = total * gain_share
    grad_tokens = (
        grad_share + inverse * (scaled - unit_share * (row_total / model_width)[None, :])
    ).astype(BF16)
    return (layer_out.T, grad_tokens.T, steer_grad)


def solution(mesh):
    split = Mesh(mesh.devices.reshape(4, 8, 2, 4, 2), SEQ + HEAD)
    placed = (
        P(SEQ, None),
        P(),
        P(SEQ, HEAD),
        P(SEQ, HEAD),
        P(SEQ, HEAD),
        P(SEQ, HEAD),
        P(),
        P(),
        P(SEQ),
        P(SEQ),
        P(SEQ, None),
    )
    return jax.shard_map(
        shards,
        mesh=split,
        in_specs=placed,
        out_specs=(P(SEQ, HEAD), P(SEQ, HEAD), P(None, HEAD)),
        check_vma=False,
    )
```

```python
import functools

import jax
import jax.numpy as jnp
from jax import lax
from jax.experimental import pallas as pl
from jax.experimental.pallas import tpu as pltpu
from jax.sharding import Mesh, PartitionSpec as P

HD = 64
WIN = 128
EPSILON = 1e-05
HIGHEST = lax.Precision.HIGHEST
SEQ = ("zh", "y", "core")
HEAD = ("x", "zl")
F32 = jnp.float32
BF16 = jnp.bfloat16
PAD = 48


def shifted(value, by):
    count = lax.axis_size(SEQ)
    pairs = [(i, i + by) for i in range(count) if 0 <= i + by < count]
    return lax.ppermute(value, SEQ, pairs)


def gathered(value, axes):
    count = lax.axis_size(axes)
    spread = jnp.broadcast_to(value[None], (count,) + value.shape)
    return lax.all_to_all(spread, axes, 0, 0)


def dot(left, right, dims, **kw):
    return lax.dot_general(left, right, (dims, ((), ())), preferred_element_type=F32, **kw)


def blocked(rows):
    width = rows.shape[-1]
    parts = rows.reshape(4, 8, 2, -1, width).transpose(1, 2, 0, 3, 4)
    parts = jnp.pad(parts, ((0, 0), (0, 0), (0, 0), (0, PAD - parts.shape[3]), (0, 0)))
    return parts.reshape(-1, width)


def unpadded(rows, row_count):
    width = rows.shape[-1]
    return rows.reshape(8, PAD, width)[:, : row_count // 8].reshape(row_count, width)


def mm(left, right, left_dim, right_dim):
    dims = (((left_dim,), (right_dim,)), ((), ()))
    return lax.dot_general(left, right, dims, preferred_element_type=F32)


def pack_kernel(q_hbm, o_hbm, k_hbm, v_hbm, out_hbm, query, out, key, value, packed, sems):
    pairs = ((q_hbm, query), (o_hbm, out), (k_hbm, key), (v_hbm, value))
    copies = start_all(pairs, sems)
    rows, width = query.shape
    packed[rows // 8 * 8 :, :] = jnp.zeros((PAD - rows // 8 * 8, packed.shape[1]), BF16)
    for copy in copies:
        copy.wait()
    packed[:rows, :width] = query[...]
    packed[:rows, width : 2 * width] = out[...]
    packed[:rows, 2 * width :] = jnp.concatenate([key[...], value[...]], axis=1)
    places = [(packed, out_hbm.at[place]) for place in range(out_hbm.shape[0])]
    for copy in start_all(places, sems):
        copy.wait()


CHUNK = 8 * PAD


def scatter_rows(blocks, row, term):
    for piece in range(CHUNK // PAD):
        number = row // PAD + piece
        z, line = number % 4, number // 4
        place = line % 8 * PAD
        group = z * 2 + line // 8
        blocks[group, place : place + PAD, :] = term[piece * PAD : (piece + 1) * PAD]


def send_blocks(blocks, blocks_hbm, sems, groups):
    sent = []
    for group in groups:
        copy = pltpu.make_async_copy(blocks.at[group], blocks_hbm.at[group], sems.at[group])
        copy.start()
        sent.append(copy)
    return sent


def start_all(pairs, sems):
    copies = [pltpu.make_async_copy(a, b, sems.at[k]) for k, (a, b) in enumerate(pairs)]
    for copy in copies:
        copy.start()
    return copies


def attend_kernel(
    w_hbm, x_hbm, g_hbm, kv_hbm, halo_hbm, mask_hbm, blocks_hbm, dq_hbm, dh_hbm, dkv_hbm, *scratch
):
    weight, normed, grads, kv, halo, mask, blocks, grad_query, grad_halo, grad_kv = scratch[:10]
    sems, out_sems = scratch[10:]
    rows_all = weight.shape[0]
    width = weight.shape[1] // 2
    together = 4
    span = together * HD
    pairs = [(x_hbm, normed)]
    for column in range(0, width, span):
        for first in (column, width + column):
            part = pl.ds(first, span)
            pairs.append((w_hbm.at[:, part], weight.at[:, part]))
        if column == 0:
            pairs.insert(2, (g_hbm, grads))
            pairs += [(kv_hbm, kv), (halo_hbm, halo), (mask_hbm, mask)]
    copies = start_all(pairs, sems)
    late = lax.broadcasted_iota(jnp.int32, (WIN, WIN), 0) > lax.broadcasted_iota(
        jnp.int32, (WIN, WIN), 1
    )
    late = jnp.concatenate([late] * together, axis=1)

    def folded(wide):
        return jnp.where(late, wide[:WIN], wide[WIN:])

    def unfolded(value):
        zero = jnp.zeros_like(value)
        parts = [jnp.where(late, value, zero), jnp.where(late, zero, value)]
        return jnp.concatenate(parts, axis=0).astype(BF16)

    def beside(rows):
        return jnp.concatenate([rows[k : k + HD] for k in range(0, span, HD)], axis=1)

    def stacked(lanes):
        return jnp.concatenate([lanes[:, k * WIN : (k + 1) * WIN] for k in range(together)], axis=0)

    grad_keys = grad_values = jnp.zeros((HD, 2 * WIN), F32)
    mixed = []
    for column in range(0, width, span):
        if column == 0:
            for copy in copies[:2]:
                copy.wait()
        else:
            copies[5 + 2 * column // span].wait()
        query = mm(weight[:, column : column + span], normed[...], 0, 0).astype(BF16)
        if column == 0:
            for copy in copies[2:7]:
                copy.wait()
            keys = jnp.concatenate([halo[:HD, :], kv[:HD, :]], axis=1)
            values = jnp.concatenate([halo[HD : 2 * HD, :], kv[HD:, :]], axis=1)
            allowed = jnp.concatenate([mask[...] > 0.0] * together, axis=1)
        else:
            copies[6 + 2 * column // span].wait()
        first = width + column
        grad = mm(weight[:, first : first + span], grads[...], 0, 0).astype(BF16)
        query, grad = beside(query), beside(grad)
        scores = folded(mm(keys, query, 0, 0)) * HD**-0.5
        scores = jnp.where(allowed, scores, -jnp.inf)
        raised = jnp.exp(scores - jnp.max(scores, axis=0, keepdims=True))
        prob = raised * (1.0 / jnp.sum(raised, axis=0, keepdims=True))
        prob_b = unfolded(prob)
        mixed.append(stacked(mm(values, prob_b, 1, 0).astype(BF16)))
        grad_values += mm(grad, prob_b, 1, 1)
        grad_prob = folded(mm(values, grad, 0, 0))
        delta = jnp.sum(prob * grad_prob, axis=0, keepdims=True)
        grad_scores = unfolded(prob * (grad_prob - delta) * HD**-0.5)
        grad_query[column : column + span, :] = stacked(mm(keys, grad_scores, 1, 0).astype(BF16))
        grad_keys += mm(query, grad_scores, 1, 1)
    grad_halo[:HD, :] = grad_keys[:, :WIN].astype(BF16)
    grad_halo[HD:, :] = grad_values[:, :WIN].astype(BF16)
    grad_kv[:HD, :] = grad_keys[:, WIN:]
    grad_kv[HD:, :] = grad_values[:, WIN:]
    results = ((grad_query, dq_hbm), (grad_halo, dh_hbm), (grad_kv, dkv_hbm))
    sent = start_all(results, out_sems.at[pl.ds(8, 3)])
    mixed = jnp.concatenate(mixed, axis=0)
    for row in range(0, rows_all, CHUNK):
        term = mm(weight[row : row + CHUNK, width:], mixed, 1, 0).astype(BF16)
        scatter_rows(blocks, row, term)
        if row + CHUNK == rows_all // 2:
            sent += send_blocks(blocks, blocks_hbm, out_sems, range(0, 8, 2))
    sent += send_blocks(blocks, blocks_hbm, out_sems, range(1, 8, 2))
    for copy in sent:
        copy.wait()


def back_kernel(w_hbm, kv_hbm, x_hbm, dq_hbm, dkv_hbm, ret_hbm, blocks_hbm, *scratch):
    weight, kv_all, normed, grad_query, grad_kv, returned, blocks, sems, out_sems = scratch
    results = ((dq_hbm, grad_query), (dkv_hbm, grad_kv), (ret_hbm, returned))
    small = start_all(results, sems.at[weight.shape[0] // (2 * CHUNK)])
    width = weight.shape[1]
    rows_all = weight.shape[0]
    size = 2 * CHUNK
    copies = []
    for step in range(rows_all // size):
        rows = pl.ds(step * size, size)
        trio = (
            (w_hbm.at[rows, pl.ds(0, width)], weight.at[rows, :]),
            (kv_hbm.at[rows, :], kv_all.at[rows, :]),
            (x_hbm.at[rows, :], normed.at[rows, :]),
        )
        copies.append(
            [pltpu.make_async_copy(a, b, sems.at[step, k]) for k, (a, b) in enumerate(trio)]
        )
        for copy in copies[-1]:
            copy.start()
    for copy in small:
        copy.wait()
    tokens_here = grad_kv.shape[1]
    kv_grad = (grad_kv[...] + returned[...].astype(F32)).astype(BF16)
    grads = grad_query[...]
    total = jnp.zeros((1, tokens_here), F32)
    for row in range(0, rows_all, CHUNK):
        if row % size == 0:
            for copy in copies[row // size]:
                copy.wait()
        rows = slice(row, row + CHUNK)
        term = mm(weight[rows, :], grads, 1, 0) + mm(kv_all[rows, :], kv_grad, 1, 0)
        term = term.astype(BF16)
        scatter_rows(blocks, row, term)
        products = term.astype(F32) * normed[rows, :].astype(F32)
        total = total + jnp.sum(products, axis=0, keepdims=True)
    high = total.astype(BF16).astype(F32)
    mid = (total - high).astype(BF16).astype(F32)
    low = total - high - mid
    line = lax.broadcasted_iota(jnp.int32, (8, tokens_here), 0)
    extra = jnp.where(line == 0, high, jnp.where(line == 1, mid, jnp.where(line == 2, low, 0.0)))
    for group in range(8):
        blocks[group, 8 * PAD :, :] = extra.astype(BF16)
    for copy in send_blocks(blocks, blocks_hbm, out_sems, range(8)):
        copy.wait()


HBM = pl.BlockSpec(memory_space=pltpu.MemorySpace.HBM)
ANY = pl.BlockSpec(memory_space=pl.ANY)


def call(kernel, outs, in_specs, out_specs, scratch, *args):
    size = sum(a.size * a.dtype.itemsize for a in jax.tree.leaves((args, outs)))
    return pl.pallas_call(
        kernel,
        out_shape=outs,
        in_specs=in_specs,
        out_specs=out_specs,
        scratch_shapes=scratch,
        compiler_params=pltpu.CompilerParams(vmem_limit_bytes=58 * 2**20),
        cost_estimate=pl.CostEstimate(flops=10**8, bytes_accessed=size, transcendentals=0),
    )(*args)


def shards(
    tokens,
    gain,
    w_query,
    w_key,
    w_value,
    w_out,
    w_gate,
    steering,
    segment_ids,
    steer_index,
    grad_out,
):
    row_count, model_width = tokens.shape
    share = model_width // 8
    start = lax.axis_index(HEAD) * share

    width = w_query.shape[1]
    like = jax.ShapeDtypeStruct
    sent = call(
        pack_kernel,
        like((4, PAD, 2 * width + 2 * HD), BF16),
        [ANY] * 4,
        HBM,
        [
            *[pltpu.VMEM(w.shape, BF16) for w in (w_query, w_out, w_key, w_value)],
            pltpu.VMEM((PAD, 2 * width + 2 * HD), BF16),
            pltpu.SemaphoreType.DMA((4,)),
        ],
        *(w_query, w_out, w_key, w_value),
    )
    near = lax.all_to_all(sent, "zh", 0, 0)
    whole = lax.all_gather(near[:, :, : 2 * width], ("y", "core"), axis=0, tiled=True)
    whole = whole.reshape(-1, 2 * width)
    kv_near = gathered(near[:, :, 2 * width :], ("y",))
    tok = tokens.T.astype(F32)
    inverse = lax.rsqrt(jnp.mean(tok * tok, axis=0, keepdims=True) + EPSILON)
    unit = tok * inverse
    normed = (unit * gain[:, None]).astype(BF16)
    normed_b = blocked(normed)
    grad_t = grad_out.T
    grad_b = blocked(grad_t)
    gate = jax.nn.sigmoid(jnp.sum(normed.astype(F32) * w_gate[:, None], axis=0))
    one_hot = steer_index[None, :] == lax.broadcasted_iota(jnp.int32, (16, row_count), 0)
    products = dot(steering, grad_t, ((1,), (0,)))
    grad_logit = gate * (1.0 - gate) * jnp.sum(jnp.where(one_hot, products, 0.0), axis=0)
    steer_share = lax.dynamic_slice_in_dim(steering, start, share, 1)
    steer_rows = dot(steer_share, one_hot.astype(BF16), ((0,), (0,)))
    grad_share = lax.dynamic_slice_in_dim(grad_t, start, share, 0).astype(F32)
    steer_part = dot(
        one_hot.astype(F32), gate[None, :] * grad_share, ((1,), (1,)), precision=HIGHEST
    )


    def exchanged(value, *steps):
        for axis, step in steps:
            pairs = [(i, i ^ step) for i in range(lax.axis_size(axis))]
            value = value + lax.ppermute(value, axis, pairs)
        return value

    steer = exchanged(steer_part, ("core", 1), ("zh", 1))
    steer, kv_near = lax.optimization_barrier((steer, kv_near))
    kv_all = lax.all_gather(kv_near[:, None], "core", axis=1, tiled=True).reshape(-1, 2 * HD)

    kv = dot(kv_all, normed_b, ((0,), (0,))).astype(BF16)
    steer, kv = lax.optimization_barrier((steer, kv))
    ids = jnp.broadcast_to(segment_ids.astype(BF16)[None], (8, row_count))
    halo = shifted(jnp.concatenate([kv, ids], axis=0), 1)
    halo_seg = halo[2 * HD].astype(jnp.int32)
    halo_seg = jnp.where(lax.axis_index(SEQ) > 0, halo_seg, -1)
    key_pos = lax.broadcasted_iota(jnp.int32, (row_count, row_count), 0)
    query_pos = lax.broadcasted_iota(jnp.int32, (row_count, row_count), 1)
    key_seg = jnp.where(key_pos > query_pos, halo_seg[:, None], segment_ids[:, None])
    mask = (key_seg == segment_ids[None, :]).astype(F32)
    steer = exchanged(steer, ("zh", 2), ("y", 1), ("y", 2))
    whole, halo, mask, steer, normed_b, grad_b, kv, kv_all = lax.optimization_barrier(
        (whole, halo, mask, steer, normed_b, grad_b, kv, kv_all)
    )
    total_rows = whole.shape[0]
    dma = pltpu.SemaphoreType.DMA
    blocks, grad_query, grad_halo, grad_kv = call(
        attend_kernel,
        (
            like((8, 8 * PAD, row_count), BF16),
            like((width, row_count), BF16),
            like((2 * HD, row_count), BF16),
            like((2 * HD, row_count), F32),
        ),
        [HBM] * 3 + [ANY] * 3,
        [HBM] + [ANY] * 3,
        [
            pltpu.VMEM((total_rows, 2 * width), BF16),
            pltpu.VMEM((total_rows, row_count), BF16),
            pltpu.VMEM((total_rows, row_count), BF16),
            pltpu.VMEM((2 * HD, row_count), BF16),
            pltpu.VMEM((2 * HD + 8, row_count), BF16),
            pltpu.VMEM((row_count, row_count), F32),
            pltpu.VMEM((8, 8 * PAD, row_count), BF16),
            pltpu.VMEM((width, row_count), BF16),
            pltpu.VMEM((2 * HD, row_count), BF16),
            pltpu.VMEM((2 * HD, row_count), F32),
            dma((9,)),
            dma((11,)),
        ],
        *(whole, normed_b, grad_b, kv, halo, mask),
    )
    returned = shifted(grad_halo, -1)
    attn = lax.all_to_all(blocks, HEAD, 0, 0)
    back = call(
        back_kernel,
        like((8, 8 * PAD + 8, row_count), BF16),
        [HBM] * 3 + [ANY] * 3,
        HBM,
        [
            pltpu.VMEM((total_rows, width), BF16),
            pltpu.VMEM((total_rows, 2 * HD), BF16),
            pltpu.VMEM((total_rows, row_count), BF16),
            pltpu.VMEM((width, row_count), BF16),
            pltpu.VMEM((2 * HD, row_count), F32),
            pltpu.VMEM((2 * HD, row_count), BF16),
            pltpu.VMEM((8, 8 * PAD + 8, row_count), BF16),
            dma((5, 3)),
            dma((8,)),
        ],
        *(whole, kv_all, normed_b, grad_query, grad_kv, returned),
    )
    steer, back = lax.optimization_barrier((steer, back))
    back = lax.all_to_all(back, HEAD, 0, 0)
    steer_grad = exchanged(steer, ("y", 4))

    attn_share = unpadded(jnp.sum(attn.astype(F32), axis=0), share)
    token_share = lax.dynamic_slice_in_dim(tokens.T, start, share, 0).astype(F32)
    layer_out = (token_share + attn_share + gate[None, :] * steer_rows).astype(BF16)
    back = jnp.sum(back.astype(F32), axis=0)
    gain_share = lax.dynamic_slice_in_dim(gain, start, share, 0)[:, None]
    gate_share = lax.dynamic_slice_in_dim(w_gate, start, share, 0)[:, None]
    total = unpadded(back[: 8 * PAD], share) + grad_logit[None, :] * gate_share
    gate_total = jnp.sum(unit * (gain * w_gate)[:, None], axis=0)
    row_total = jnp.sum(back[8 * PAD : 8 * PAD + 3], axis=0) + grad_logit * gate_total
    unit_share = token_share * inverse
    scaled = total * gain_share
    grad_tokens = (
        grad_share + inverse * (scaled - unit_share * (row_total / model_width)[None, :])
    ).astype(BF16)
    return (layer_out.T, grad_tokens.T, steer_grad)


def solution(mesh):
    split = Mesh(mesh.devices.reshape(4, 8, 2, 4, 2), SEQ + HEAD)
    placed = (
        P(SEQ, None),
        P(),
        P(SEQ, HEAD),
        P(SEQ, HEAD),
        P(SEQ, HEAD),
        P(SEQ, HEAD),
        P(),
        P(),
        P(SEQ),
        P(SEQ),
        P(SEQ, None),
    )
    return jax.shard_map(
        shards,
        mesh=split,
        in_specs=placed,
        out_specs=(P(SEQ, HEAD), P(SEQ, HEAD), P(None, HEAD)),
        check_vma=False,
    )
```

```python
import functools

import jax
import jax.numpy as jnp
from jax import lax
from jax.experimental import pallas as pl
from jax.experimental.pallas import tpu as pltpu
from jax.sharding import Mesh, PartitionSpec as P

HD = 64
WIN = 128
EPSILON = 1e-05
HIGHEST = lax.Precision.HIGHEST
SEQ = ("zh", "y", "core")
HEAD = ("x", "zl")
F32 = jnp.float32
BF16 = jnp.bfloat16
PAD = 48


def shifted(value, by):
    count = lax.axis_size(SEQ)
    pairs = [(i, i + by) for i in range(count) if 0 <= i + by < count]
    return lax.ppermute(value, SEQ, pairs)


def gathered(value, axes):
    count = lax.axis_size(axes)
    spread = jnp.broadcast_to(value[None], (count,) + value.shape)
    return lax.all_to_all(spread, axes, 0, 0)


def dot(left, right, dims, **kw):
    return lax.dot_general(left, right, (dims, ((), ())), preferred_element_type=F32, **kw)


def blocked(rows):
    width = rows.shape[-1]
    parts = rows.reshape(4, 8, 2, -1, width).transpose(1, 2, 0, 3, 4)
    parts = jnp.pad(parts, ((0, 0), (0, 0), (0, 0), (0, PAD - parts.shape[3]), (0, 0)))
    return parts.reshape(-1, width)


def unpadded(rows, row_count):
    width = rows.shape[-1]
    return rows.reshape(8, PAD, width)[:, : row_count // 8].reshape(row_count, width)


def mm(left, right, left_dim, right_dim):
    dims = (((left_dim,), (right_dim,)), ((), ()))
    return lax.dot_general(left, right, dims, preferred_element_type=F32)


def pack_kernel(q_hbm, o_hbm, k_hbm, v_hbm, out_hbm, query, out, key, value, packed, sems):
    pairs = ((q_hbm, query), (o_hbm, out), (k_hbm, key), (v_hbm, value))
    copies = start_all(pairs, sems)
    rows, width = query.shape
    packed[rows // 8 * 8 :, :] = jnp.zeros((PAD - rows // 8 * 8, packed.shape[1]), BF16)
    for copy in copies:
        copy.wait()
    packed[:rows, :width] = query[...]
    packed[:rows, width : 2 * width] = out[...]
    packed[:rows, 2 * width :] = jnp.concatenate([key[...], value[...]], axis=1)
    places = [(packed, out_hbm.at[place]) for place in range(out_hbm.shape[0])]
    for copy in start_all(places, sems):
        copy.wait()


CHUNK = 8 * PAD


def scatter_rows(blocks, row, term):
    for piece in range(CHUNK // PAD):
        number = row // PAD + piece
        z, line = number % 4, number // 4
        place = line % 8 * PAD
        group = z * 2 + line // 8
        blocks[group, place : place + PAD, :] = term[piece * PAD : (piece + 1) * PAD]


def send_blocks(blocks, blocks_hbm, sems, groups):
    sent = []
    for group in groups:
        copy = pltpu.make_async_copy(blocks.at[group], blocks_hbm.at[group], sems.at[group])
        copy.start()
        sent.append(copy)
    return sent


def start_all(pairs, sems):
    copies = [pltpu.make_async_copy(a, b, sems.at[k]) for k, (a, b) in enumerate(pairs)]
    for copy in copies:
        copy.start()
    return copies


def attend_kernel(
    w_hbm, x_hbm, g_hbm, kv_hbm, halo_hbm, mask_hbm, blocks_hbm, dq_hbm, dh_hbm, dkv_hbm, *scratch
):
    weight, normed, grads, kv, halo, mask, blocks, grad_query, grad_halo, grad_kv = scratch[:10]
    sems, out_sems = scratch[10:]
    rows_all = weight.shape[0]
    width = weight.shape[1] // 2
    together = 4
    span = together * HD
    pairs = [(x_hbm, normed)]
    for column in range(0, width, span):
        for first in (column, width + column):
            part = pl.ds(first, span)
            pairs.append((w_hbm.at[:, part], weight.at[:, part]))
        if column == 0:
            pairs.insert(2, (g_hbm, grads))
            pairs += [(kv_hbm, kv), (halo_hbm, halo), (mask_hbm, mask)]
    copies = start_all(pairs, sems)
    late = lax.broadcasted_iota(jnp.int32, (WIN, WIN), 0) > lax.broadcasted_iota(
        jnp.int32, (WIN, WIN), 1
    )
    late = jnp.concatenate([late] * together, axis=1)

    def folded(wide):
        return jnp.where(late, wide[:WIN], wide[WIN:])

    def unfolded(value):
        zero = jnp.zeros_like(value)
        parts = [jnp.where(late, value, zero), jnp.where(late, zero, value)]
        return jnp.concatenate(parts, axis=0).astype(BF16)

    def beside(rows):
        return jnp.concatenate([rows[k : k + HD] for k in range(0, span, HD)], axis=1)

    def stacked(lanes):
        return jnp.concatenate([lanes[:, k * WIN : (k + 1) * WIN] for k in range(together)], axis=0)

    grad_keys = grad_values = jnp.zeros((HD, 2 * WIN), F32)
    mixed = []
    for column in range(0, width, span):
        if column == 0:
            for copy in copies[:2]:
                copy.wait()
        else:
            copies[5 + 2 * column // span].wait()
        query = mm(weight[:, column : column + span], normed[...], 0, 0).astype(BF16)
        if column == 0:
            for copy in copies[2:7]:
                copy.wait()
            keys = jnp.concatenate([halo[:HD, :], kv[:HD, :]], axis=1)
            values = jnp.concatenate([halo[HD : 2 * HD, :], kv[HD:, :]], axis=1)
            allowed = jnp.concatenate([mask[...] > 0.0] * together, axis=1)
        else:
            copies[6 + 2 * column // span].wait()
        first = width + column
        grad = mm(weight[:, first : first + span], grads[...], 0, 0).astype(BF16)
        query, grad = beside(query), beside(grad)
        scores = folded(mm(keys, query, 0, 0)) * HD**-0.5
        scores = jnp.where(allowed, scores, -jnp.inf)
        raised = jnp.exp(scores - jnp.max(scores, axis=0, keepdims=True))
        prob = raised * (1.0 / jnp.sum(raised, axis=0, keepdims=True))
        prob_b = unfolded(prob)
        mixed.append(stacked(mm(values, prob_b, 1, 0).astype(BF16)))
        grad_values += mm(grad, prob_b, 1, 1)
        grad_prob = folded(mm(values, grad, 0, 0))
        delta = jnp.sum(prob * grad_prob, axis=0, keepdims=True)
        grad_scores = unfolded(prob * (grad_prob - delta) * HD**-0.5)
        grad_query[column : column + span, :] = stacked(mm(keys, grad_scores, 1, 0).astype(BF16))
        grad_keys += mm(query, grad_scores, 1, 1)
    grad_halo[:HD, :] = grad_keys[:, :WIN].astype(BF16)
    grad_halo[HD:, :] = grad_values[:, :WIN].astype(BF16)
    grad_kv[:HD, :] = grad_keys[:, WIN:]
    grad_kv[HD:, :] = grad_values[:, WIN:]
    results = ((grad_query, dq_hbm), (grad_halo, dh_hbm), (grad_kv, dkv_hbm))
    sent = start_all(results, out_sems.at[pl.ds(8, 3)])
    mixed = jnp.concatenate(mixed, axis=0)
    for row in range(0, rows_all, CHUNK):
        term = mm(weight[row : row + CHUNK, width:], mixed, 1, 0).astype(BF16)
        scatter_rows(blocks, row, term)
        if row + CHUNK == rows_all // 2:
            sent += send_blocks(blocks, blocks_hbm, out_sems, range(0, 8, 2))
    sent += send_blocks(blocks, blocks_hbm, out_sems, range(1, 8, 2))
    for copy in sent:
        copy.wait()


def back_kernel(w_hbm, kv_hbm, x_hbm, dq_hbm, dkv_hbm, ret_hbm, blocks_hbm, *scratch):
    weight, kv_all, normed, grad_query, grad_kv, returned, blocks, sems, out_sems = scratch
    results = ((dq_hbm, grad_query), (dkv_hbm, grad_kv), (ret_hbm, returned))
    small = start_all(results, sems.at[weight.shape[0] // (2 * CHUNK)])
    width = weight.shape[1]
    rows_all = weight.shape[0]
    size = 2 * CHUNK
    copies = []
    for step in range(rows_all // size):
        rows = pl.ds(step * size, size)
        trio = (
            (w_hbm.at[rows, pl.ds(0, width)], weight.at[rows, :]),
            (kv_hbm.at[rows, :], kv_all.at[rows, :]),
            (x_hbm.at[rows, :], normed.at[rows, :]),
        )
        copies.append(
            [pltpu.make_async_copy(a, b, sems.at[step, k]) for k, (a, b) in enumerate(trio)]
        )
        for copy in copies[-1]:
            copy.start()
    for copy in small:
        copy.wait()
    tokens_here = grad_kv.shape[1]
    kv_grad = (grad_kv[...] + returned[...].astype(F32)).astype(BF16)
    grads = grad_query[...]
    total = jnp.zeros((1, tokens_here), F32)
    for row in range(0, rows_all, CHUNK):
        if row % size == 0:
            for copy in copies[row // size]:
                copy.wait()
        rows = slice(row, row + CHUNK)
        term = mm(weight[rows, :], grads, 1, 0) + mm(kv_all[rows, :], kv_grad, 1, 0)
        term = term.astype(BF16)
        scatter_rows(blocks, row, term)
        products = term.astype(F32) * normed[rows, :].astype(F32)
        total = total + jnp.sum(products, axis=0, keepdims=True)
    high = total.astype(BF16).astype(F32)
    mid = (total - high).astype(BF16).astype(F32)
    low = total - high - mid
    line = lax.broadcasted_iota(jnp.int32, (8, tokens_here), 0)
    extra = jnp.where(line == 0, high, jnp.where(line == 1, mid, jnp.where(line == 2, low, 0.0)))
    for group in range(8):
        blocks[group, 8 * PAD :, :] = extra.astype(BF16)
    for copy in send_blocks(blocks, blocks_hbm, out_sems, range(8)):
        copy.wait()


HBM = pl.BlockSpec(memory_space=pltpu.MemorySpace.HBM)
ANY = pl.BlockSpec(memory_space=pl.ANY)


def call(kernel, outs, in_specs, out_specs, scratch, *args):
    limit = 48 if kernel is back_kernel else 58
    size = sum(a.size * a.dtype.itemsize for a in jax.tree.leaves((args, outs)))
    return pl.pallas_call(
        kernel,
        out_shape=outs,
        in_specs=in_specs,
        out_specs=out_specs,
        scratch_shapes=scratch,
        compiler_params=pltpu.CompilerParams(vmem_limit_bytes=limit * 2**20),
        cost_estimate=pl.CostEstimate(flops=10**8, bytes_accessed=size, transcendentals=0),
    )(*args)


def shards(
    tokens,
    gain,
    w_query,
    w_key,
    w_value,
    w_out,
    w_gate,
    steering,
    segment_ids,
    steer_index,
    grad_out,
):
    row_count, model_width = tokens.shape
    share = model_width // 8
    start = lax.axis_index(HEAD) * share

    width = w_query.shape[1]
    like = jax.ShapeDtypeStruct
    sent = call(
        pack_kernel,
        like((4, PAD, 2 * width + 2 * HD), BF16),
        [ANY] * 4,
        HBM,
        [
            *[pltpu.VMEM(w.shape, BF16) for w in (w_query, w_out, w_key, w_value)],
            pltpu.VMEM((PAD, 2 * width + 2 * HD), BF16),
            pltpu.SemaphoreType.DMA((4,)),
        ],
        *(w_query, w_out, w_key, w_value),
    )
    near = lax.all_to_all(sent, "zh", 0, 0)
    whole = lax.all_gather(near[:, :, : 2 * width], ("y", "core"), axis=0, tiled=True)
    whole = whole.reshape(-1, 2 * width)
    kv_near = gathered(near[:, :, 2 * width :], ("y",))
    tok = tokens.T.astype(F32)
    inverse = lax.rsqrt(jnp.mean(tok * tok, axis=0, keepdims=True) + EPSILON)
    unit = tok * inverse
    normed = (unit * gain[:, None]).astype(BF16)
    normed_b = blocked(normed)
    grad_t = grad_out.T
    grad_b = blocked(grad_t)
    gate = jax.nn.sigmoid(jnp.sum(normed.astype(F32) * w_gate[:, None], axis=0))
    one_hot = steer_index[None, :] == lax.broadcasted_iota(jnp.int32, (16, row_count), 0)
    products = dot(steering, grad_t, ((1,), (0,)))
    grad_logit = gate * (1.0 - gate) * jnp.sum(jnp.where(one_hot, products, 0.0), axis=0)
    steer_share = lax.dynamic_slice_in_dim(steering, start, share, 1)
    steer_rows = dot(steer_share, one_hot.astype(BF16), ((0,), (0,)))
    grad_share = lax.dynamic_slice_in_dim(grad_t, start, share, 0).astype(F32)
    steer_part = dot(
        one_hot.astype(F32), gate[None, :] * grad_share, ((1,), (1,)), precision=HIGHEST
    )


    def exchanged(value, *steps):
        for axis, step in steps:
            pairs = [(i, i ^ step) for i in range(lax.axis_size(axis))]
            value = value + lax.ppermute(value, axis, pairs)
        return value

    steer = exchanged(steer_part, ("core", 1), ("zh", 1))
    steer, kv_near = lax.optimization_barrier((steer, kv_near))
    kv_all = lax.all_gather(kv_near[:, None], "core", axis=1, tiled=True).reshape(-1, 2 * HD)

    kv = dot(kv_all, normed_b, ((0,), (0,))).astype(BF16)
    steer, kv = lax.optimization_barrier((steer, kv))
    ids = jnp.broadcast_to(segment_ids.astype(BF16)[None], (8, row_count))
    halo = shifted(jnp.concatenate([kv, ids], axis=0), 1)
    halo_seg = halo[2 * HD].astype(jnp.int32)
    halo_seg = jnp.where(lax.axis_index(SEQ) > 0, halo_seg, -1)
    key_pos = lax.broadcasted_iota(jnp.int32, (row_count, row_count), 0)
    query_pos = lax.broadcasted_iota(jnp.int32, (row_count, row_count), 1)
    key_seg = jnp.where(key_pos > query_pos, halo_seg[:, None], segment_ids[:, None])
    mask = (key_seg == segment_ids[None, :]).astype(F32)
    steer = exchanged(steer, ("zh", 2), ("y", 1))
    whole, halo, mask, steer, normed_b, grad_b, kv, kv_all = lax.optimization_barrier(
        (whole, halo, mask, steer, normed_b, grad_b, kv, kv_all)
    )
    total_rows = whole.shape[0]
    dma = pltpu.SemaphoreType.DMA
    blocks, grad_query, grad_halo, grad_kv = call(
        attend_kernel,
        (
            like((8, 8 * PAD, row_count), BF16),
            like((width, row_count), BF16),
            like((2 * HD, row_count), BF16),
            like((2 * HD, row_count), F32),
        ),
        [HBM] * 3 + [ANY] * 3,
        [HBM] + [ANY] * 3,
        [
            pltpu.VMEM((total_rows, 2 * width), BF16),
            pltpu.VMEM((total_rows, row_count), BF16),
            pltpu.VMEM((total_rows, row_count), BF16),
            pltpu.VMEM((2 * HD, row_count), BF16),
            pltpu.VMEM((2 * HD + 8, row_count), BF16),
            pltpu.VMEM((row_count, row_count), F32),
            pltpu.VMEM((8, 8 * PAD, row_count), BF16),
            pltpu.VMEM((width, row_count), BF16),
            pltpu.VMEM((2 * HD, row_count), BF16),
            pltpu.VMEM((2 * HD, row_count), F32),
            dma((9,)),
            dma((11,)),
        ],
        *(whole, normed_b, grad_b, kv, halo, mask),
    )
    returned = shifted(grad_halo, -1)
    steer, returned = lax.optimization_barrier((steer, returned))
    steer = exchanged(steer, ("y", 2))
    attn = lax.all_to_all(blocks, HEAD, 0, 0)
    back = call(
        back_kernel,
        like((8, 8 * PAD + 8, row_count), BF16),
        [HBM] * 3 + [ANY] * 3,
        HBM,
        [
            pltpu.VMEM((total_rows, width), BF16),
            pltpu.VMEM((total_rows, 2 * HD), BF16),
            pltpu.VMEM((total_rows, row_count), BF16),
            pltpu.VMEM((width, row_count), BF16),
            pltpu.VMEM((2 * HD, row_count), F32),
            pltpu.VMEM((2 * HD, row_count), BF16),
            pltpu.VMEM((8, 8 * PAD + 8, row_count), BF16),
            dma((5, 3)),
            dma((8,)),
        ],
        *(whole, kv_all, normed_b, grad_query, grad_kv, returned),
    )
    steer, back = lax.optimization_barrier((steer, back))
    back = lax.all_to_all(back, HEAD, 0, 0)
    steer_grad = exchanged(steer, ("y", 4))

    attn_share = unpadded(jnp.sum(attn.astype(F32), axis=0), share)
    token_share = lax.dynamic_slice_in_dim(tokens.T, start, share, 0).astype(F32)
    layer_out = (token_share + attn_share + gate[None, :] * steer_rows).astype(BF16)
    back = jnp.sum(back.astype(F32), axis=0)
    gain_share = lax.dynamic_slice_in_dim(gain, start, share, 0)[:, None]
    gate_share = lax.dynamic_slice_in_dim(w_gate, start, share, 0)[:, None]
    total = unpadded(back[: 8 * PAD], share) + grad_logit[None, :] * gate_share
    gate_total = jnp.sum(unit * (gain * w_gate)[:, None], axis=0)
    row_total = jnp.sum(back[8 * PAD : 8 * PAD + 3], axis=0) + grad_logit * gate_total
    unit_share = token_share * inverse
    scaled = total * gain_share
    grad_tokens = (
        grad_share + inverse * (scaled - unit_share * (row_total / model_width)[None, :])
    ).astype(BF16)
    return (layer_out.T, grad_tokens.T, steer_grad)


def solution(mesh):
    split = Mesh(mesh.devices.reshape(4, 8, 2, 4, 2), SEQ + HEAD)
    placed = (
        P(SEQ, None),
        P(),
        P(SEQ, HEAD),
        P(SEQ, HEAD),
        P(SEQ, HEAD),
        P(SEQ, HEAD),
        P(),
        P(),
        P(SEQ),
        P(SEQ),
        P(SEQ, None),
    )
    return jax.shard_map(
        shards,
        mesh=split,
        in_specs=placed,
        out_specs=(P(SEQ, HEAD), P(SEQ, HEAD), P(None, HEAD)),
        check_vma=False,
    )
```

```python
import functools

import jax
import jax.numpy as jnp
from jax import lax
from jax.experimental import pallas as pl
from jax.experimental.pallas import tpu as pltpu
from jax.sharding import Mesh, PartitionSpec as P

HD = 64
WIN = 128
EPSILON = 1e-05
HIGHEST = lax.Precision.HIGHEST
SEQ = ("zh", "y", "core")
HEAD = ("x", "zl")
F32 = jnp.float32
BF16 = jnp.bfloat16
PAD = 48


def shifted(value, by):
    count = lax.axis_size(SEQ)
    pairs = [(i, i + by) for i in range(count) if 0 <= i + by < count]
    return lax.ppermute(value, SEQ, pairs)


def gathered(value, axes):
    count = lax.axis_size(axes)
    spread = jnp.broadcast_to(value[None], (count,) + value.shape)
    return lax.all_to_all(spread, axes, 0, 0)


def dot(left, right, dims, **kw):
    return lax.dot_general(left, right, (dims, ((), ())), preferred_element_type=F32, **kw)


def blocked(rows):
    width = rows.shape[-1]
    parts = rows.reshape(4, 8, 2, -1, width).transpose(1, 2, 0, 3, 4)
    parts = jnp.pad(parts, ((0, 0), (0, 0), (0, 0), (0, PAD - parts.shape[3]), (0, 0)))
    return parts.reshape(-1, width)


def unpadded(rows, row_count):
    width = rows.shape[-1]
    return rows.reshape(8, PAD, width)[:, : row_count // 8].reshape(row_count, width)


def mm(left, right, left_dim, right_dim):
    dims = (((left_dim,), (right_dim,)), ((), ()))
    return lax.dot_general(left, right, dims, preferred_element_type=F32)


def pack_kernel(q_hbm, o_hbm, k_hbm, v_hbm, out_hbm, query, out, key, value, packed, sems):
    pairs = ((q_hbm, query), (o_hbm, out), (k_hbm, key), (v_hbm, value))
    copies = start_all(pairs, sems)
    rows, width = query.shape
    packed[rows // 8 * 8 :, :] = jnp.zeros((PAD - rows // 8 * 8, packed.shape[1]), BF16)
    for copy in copies:
        copy.wait()
    packed[:rows, :width] = query[...]
    packed[:rows, width : 2 * width] = out[...]
    packed[:rows, 2 * width :] = jnp.concatenate([key[...], value[...]], axis=1)
    places = [(packed, out_hbm.at[place]) for place in range(out_hbm.shape[0])]
    for copy in start_all(places, sems):
        copy.wait()


CHUNK = 8 * PAD


def scatter_rows(blocks, row, term):
    for piece in range(CHUNK // PAD):
        number = row // PAD + piece
        z, line = number % 4, number // 4
        place = line % 8 * PAD
        group = z * 2 + line // 8
        blocks[group, place : place + PAD, :] = term[piece * PAD : (piece + 1) * PAD]


def send_blocks(blocks, blocks_hbm, sems, groups):
    sent = []
    for group in groups:
        copy = pltpu.make_async_copy(blocks.at[group], blocks_hbm.at[group], sems.at[group])
        copy.start()
        sent.append(copy)
    return sent


def start_all(pairs, sems):
    copies = [pltpu.make_async_copy(a, b, sems.at[k]) for k, (a, b) in enumerate(pairs)]
    for copy in copies:
        copy.start()
    return copies


def attend_kernel(
    w_hbm, x_hbm, g_hbm, kv_hbm, halo_hbm, mask_hbm, blocks_hbm, dq_hbm, dh_hbm, dkv_hbm, *scratch
):
    weight, normed, grads, kv, halo, mask, blocks, grad_query, grad_halo, grad_kv = scratch[:10]
    sems, out_sems = scratch[10:]
    rows_all = weight.shape[0]
    width = weight.shape[1] // 2
    together = 4
    span = together * HD
    pairs = [(x_hbm, normed)]
    for column in range(0, width, span):
        for first in (column, width + column):
            part = pl.ds(first, span)
            pairs.append((w_hbm.at[:, part], weight.at[:, part]))
        if column == 0:
            pairs.insert(2, (g_hbm, grads))
            pairs += [(kv_hbm, kv), (halo_hbm, halo), (mask_hbm, mask)]
    copies = start_all(pairs, sems)
    late = lax.broadcasted_iota(jnp.int32, (WIN, WIN), 0) > lax.broadcasted_iota(
        jnp.int32, (WIN, WIN), 1
    )
    late = jnp.concatenate([late] * together, axis=1)

    def folded(wide):
        return jnp.where(late, wide[:WIN], wide[WIN:])

    def unfolded(value):
        zero = jnp.zeros_like(value)
        parts = [jnp.where(late, value, zero), jnp.where(late, zero, value)]
        return jnp.concatenate(parts, axis=0).astype(BF16)

    def beside(rows):
        return jnp.concatenate([rows[k : k + HD] for k in range(0, span, HD)], axis=1)

    def stacked(lanes):
        return jnp.concatenate([lanes[:, k * WIN : (k + 1) * WIN] for k in range(together)], axis=0)

    grad_keys = grad_values = jnp.zeros((HD, 2 * WIN), F32)
    mixed = []
    for column in range(0, width, span):
        if column == 0:
            for copy in copies[:2]:
                copy.wait()
        else:
            copies[5 + 2 * column // span].wait()
        query = mm(weight[:, column : column + span], normed[...], 0, 0).astype(BF16)
        if column == 0:
            for copy in copies[2:7]:
                copy.wait()
            keys = jnp.concatenate([halo[:HD, :], kv[:HD, :]], axis=1)
            values = jnp.concatenate([halo[HD : 2 * HD, :], kv[HD:, :]], axis=1)
            allowed = jnp.concatenate([mask[...] > 0.0] * together, axis=1)
        else:
            copies[6 + 2 * column // span].wait()
        first = width + column
        grad = mm(weight[:, first : first + span], grads[...], 0, 0).astype(BF16)
        query, grad = beside(query), beside(grad)
        scores = folded(mm(keys, query, 0, 0)) * HD**-0.5
        scores = jnp.where(allowed, scores, -jnp.inf)
        raised = jnp.exp(scores - jnp.max(scores, axis=0, keepdims=True))
        prob = raised * (1.0 / jnp.sum(raised, axis=0, keepdims=True))
        prob_b = unfolded(prob)
        mixed.append(stacked(mm(values, prob_b, 1, 0).astype(BF16)))
        grad_values += mm(grad, prob_b, 1, 1)
        grad_prob = folded(mm(values, grad, 0, 0))
        delta = jnp.sum(prob * grad_prob, axis=0, keepdims=True)
        grad_scores = unfolded(prob * (grad_prob - delta) * HD**-0.5)
        grad_query[column : column + span, :] = stacked(mm(keys, grad_scores, 1, 0).astype(BF16))
        grad_keys += mm(query, grad_scores, 1, 1)
    grad_halo[:HD, :] = grad_keys[:, :WIN].astype(BF16)
    grad_halo[HD:, :] = grad_values[:, :WIN].astype(BF16)
    grad_kv[:HD, :] = grad_keys[:, WIN:]
    grad_kv[HD:, :] = grad_values[:, WIN:]
    results = ((grad_query, dq_hbm), (grad_halo, dh_hbm), (grad_kv, dkv_hbm))
    sent = start_all(results, out_sems.at[pl.ds(8, 3)])
    mixed = jnp.concatenate(mixed, axis=0)
    for row in range(0, rows_all, CHUNK):
        term = mm(weight[row : row + CHUNK, width:], mixed, 1, 0).astype(BF16)
        scatter_rows(blocks, row, term)
        if row + CHUNK == rows_all // 2:
            sent += send_blocks(blocks, blocks_hbm, out_sems, range(0, 8, 2))
    sent += send_blocks(blocks, blocks_hbm, out_sems, range(1, 8, 2))
    for copy in sent:
        copy.wait()


def back_kernel(w_hbm, kv_hbm, x_hbm, dq_hbm, dkv_hbm, ret_hbm, blocks_hbm, *scratch):
    weight, kv_all, normed, grad_query, grad_kv, returned, blocks, sems, out_sems = scratch
    results = ((dq_hbm, grad_query), (dkv_hbm, grad_kv), (ret_hbm, returned))
    small = start_all(results, sems.at[weight.shape[0] // (2 * CHUNK)])
    width = weight.shape[1]
    rows_all = weight.shape[0]
    size = 2 * CHUNK
    copies = []
    for step in range(rows_all // size):
        rows = pl.ds(step * size, size)
        trio = (
            (w_hbm.at[rows, pl.ds(0, width)], weight.at[rows, :]),
            (kv_hbm.at[rows, :], kv_all.at[rows, :]),
            (x_hbm.at[rows, :], normed.at[rows, :]),
        )
        copies.append(
            [pltpu.make_async_copy(a, b, sems.at[step, k]) for k, (a, b) in enumerate(trio)]
        )
        for copy in copies[-1]:
            copy.start()
    for copy in small:
        copy.wait()
    tokens_here = grad_kv.shape[1]
    kv_grad = (grad_kv[...] + returned[...].astype(F32)).astype(BF16)
    grads = grad_query[...]
    total = jnp.zeros((1, tokens_here), F32)
    for row in range(0, rows_all, CHUNK):
        if row % size == 0:
            for copy in copies[row // size]:
                copy.wait()
        rows = slice(row, row + CHUNK)
        term = mm(weight[rows, :], grads, 1, 0) + mm(kv_all[rows, :], kv_grad, 1, 0)
        term = term.astype(BF16)
        scatter_rows(blocks, row, term)
        products = term.astype(F32) * normed[rows, :].astype(F32)
        total = total + jnp.sum(products, axis=0, keepdims=True)
    high = total.astype(BF16).astype(F32)
    mid = (total - high).astype(BF16).astype(F32)
    low = total - high - mid
    line = lax.broadcasted_iota(jnp.int32, (8, tokens_here), 0)
    extra = jnp.where(line == 0, high, jnp.where(line == 1, mid, jnp.where(line == 2, low, 0.0)))
    for group in range(8):
        blocks[group, 8 * PAD :, :] = extra.astype(BF16)
    for copy in send_blocks(blocks, blocks_hbm, out_sems, range(8)):
        copy.wait()


HBM = pl.BlockSpec(memory_space=pltpu.MemorySpace.HBM)
ANY = pl.BlockSpec(memory_space=pl.ANY)


def call(kernel, outs, in_specs, out_specs, scratch, *args):
    size = sum(a.size * a.dtype.itemsize for a in jax.tree.leaves((args, outs)))
    return pl.pallas_call(
        kernel,
        out_shape=outs,
        in_specs=in_specs,
        out_specs=out_specs,
        scratch_shapes=scratch,
        compiler_params=pltpu.CompilerParams(vmem_limit_bytes=58 * 2**20),
        cost_estimate=pl.CostEstimate(flops=10**8, bytes_accessed=size, transcendentals=0),
    )(*args)


def shards(
    tokens,
    gain,
    w_query,
    w_key,
    w_value,
    w_out,
    w_gate,
    steering,
    segment_ids,
    steer_index,
    grad_out,
):
    row_count, model_width = tokens.shape
    share = model_width // 8
    start = lax.axis_index(HEAD) * share

    width = w_query.shape[1]
    like = jax.ShapeDtypeStruct
    sent = call(
        pack_kernel,
        like((4, PAD, 2 * width + 2 * HD), BF16),
        [ANY] * 4,
        HBM,
        [
            *[pltpu.VMEM(w.shape, BF16) for w in (w_query, w_out, w_key, w_value)],
            pltpu.VMEM((PAD, 2 * width + 2 * HD), BF16),
            pltpu.SemaphoreType.DMA((4,)),
        ],
        *(w_query, w_out, w_key, w_value),
    )
    near = lax.all_to_all(sent, "zh", 0, 0)
    whole = lax.all_gather(near[:, :, : 2 * width], ("y", "core"), axis=0, tiled=True)
    whole = whole.reshape(-1, 2 * width)
    kv_near = gathered(near[:, :, 2 * width :], ("y",))
    tok = tokens.T.astype(F32)
    inverse = lax.rsqrt(jnp.mean(tok * tok, axis=0, keepdims=True) + EPSILON)
    unit = tok * inverse
    normed = (unit * gain[:, None]).astype(BF16)
    normed_b = blocked(normed)
    grad_t = grad_out.T
    grad_b = blocked(grad_t)
    gate = jax.nn.sigmoid(jnp.sum(normed.astype(F32) * w_gate[:, None], axis=0))
    one_hot = steer_index[None, :] == lax.broadcasted_iota(jnp.int32, (16, row_count), 0)
    products = dot(steering, grad_t, ((1,), (0,)))
    grad_logit = gate * (1.0 - gate) * jnp.sum(jnp.where(one_hot, products, 0.0), axis=0)
    steer_share = lax.dynamic_slice_in_dim(steering, start, share, 1)
    steer_rows = dot(steer_share, one_hot.astype(BF16), ((0,), (0,)))
    grad_share = lax.dynamic_slice_in_dim(grad_t, start, share, 0).astype(F32)
    steer_part = dot(
        one_hot.astype(F32), gate[None, :] * grad_share, ((1,), (1,)), precision=HIGHEST
    )


    def exchanged(value, *steps):
        for axis, step in steps:
            pairs = [(i, i ^ step) for i in range(lax.axis_size(axis))]
            value = value + lax.ppermute(value, axis, pairs)
        return value

    steer = exchanged(steer_part, ("core", 1), ("zh", 1))
    steer, kv_near = lax.optimization_barrier((steer, kv_near))
    kv_all = lax.all_gather(kv_near[:, None], "core", axis=1, tiled=True).reshape(-1, 2 * HD)

    kv = dot(kv_all, normed_b, ((0,), (0,))).astype(BF16)
    steer, kv = lax.optimization_barrier((steer, kv))
    ids = jnp.broadcast_to(segment_ids.astype(BF16)[None], (8, row_count))
    halo = shifted(jnp.concatenate([kv, ids], axis=0), 1)
    halo_seg = halo[2 * HD].astype(jnp.int32)
    halo_seg = jnp.where(lax.axis_index(SEQ) > 0, halo_seg, -1)
    key_pos = lax.broadcasted_iota(jnp.int32, (row_count, row_count), 0)
    query_pos = lax.broadcasted_iota(jnp.int32, (row_count, row_count), 1)
    key_seg = jnp.where(key_pos > query_pos, halo_seg[:, None], segment_ids[:, None])
    mask = (key_seg == segment_ids[None, :]).astype(F32)
    steer = exchanged(steer, ("zh", 2), ("y", 1))
    whole, halo, mask, steer, normed_b, grad_b, kv, kv_all = lax.optimization_barrier(
        (whole, halo, mask, steer, normed_b, grad_b, kv, kv_all)
    )
    total_rows = whole.shape[0]
    dma = pltpu.SemaphoreType.DMA
    blocks, grad_query, grad_halo, grad_kv = call(
        attend_kernel,
        (
            like((8, 8 * PAD, row_count), BF16),
            like((width, row_count), BF16),
            like((2 * HD, row_count), BF16),
            like((2 * HD, row_count), F32),
        ),
        [HBM] * 3 + [ANY] * 3,
        [HBM] + [ANY] * 3,
        [
            pltpu.VMEM((total_rows, 2 * width), BF16),
            pltpu.VMEM((total_rows, row_count), BF16),
            pltpu.VMEM((total_rows, row_count), BF16),
            pltpu.VMEM((2 * HD, row_count), BF16),
            pltpu.VMEM((2 * HD + 8, row_count), BF16),
            pltpu.VMEM((row_count, row_count), F32),
            pltpu.VMEM((8, 8 * PAD, row_count), BF16),
            pltpu.VMEM((width, row_count), BF16),
            pltpu.VMEM((2 * HD, row_count), BF16),
            pltpu.VMEM((2 * HD, row_count), F32),
            dma((9,)),
            dma((11,)),
        ],
        *(whole, normed_b, grad_b, kv, halo, mask),
    )
    returned = shifted(grad_halo, -1)
    steer, returned = lax.optimization_barrier((steer, returned))
    steer = exchanged(steer, ("y", 2))
    attn = lax.all_to_all(blocks, HEAD, 0, 0)
    back = call(
        back_kernel,
        like((8, 8 * PAD + 8, row_count), BF16),
        [HBM] * 3 + [ANY] * 3,
        HBM,
        [
            pltpu.VMEM((total_rows, width), BF16),
            pltpu.VMEM((total_rows, 2 * HD), BF16),
            pltpu.VMEM((total_rows, row_count), BF16),
            pltpu.VMEM((width, row_count), BF16),
            pltpu.VMEM((2 * HD, row_count), F32),
            pltpu.VMEM((2 * HD, row_count), BF16),
            pltpu.VMEM((8, 8 * PAD + 8, row_count), BF16),
            dma((5, 3)),
            dma((8,)),
        ],
        *(whole, kv_all, normed_b, grad_query, grad_kv, returned),
    )
    steer, back = lax.optimization_barrier((steer, back))
    back = lax.all_to_all(back, HEAD, 0, 0)
    steer_grad = exchanged(steer, ("y", 4))

    attn_share = unpadded(jnp.sum(attn.astype(F32), axis=0), share)
    token_share = lax.dynamic_slice_in_dim(tokens.T, start, share, 0).astype(F32)
    layer_out = (token_share + attn_share + gate[None, :] * steer_rows).astype(BF16)
    back = jnp.sum(back.astype(F32), axis=0)
    gain_share = lax.dynamic_slice_in_dim(gain, start, share, 0)[:, None]
    gate_share = lax.dynamic_slice_in_dim(w_gate, start, share, 0)[:, None]
    total = unpadded(back[: 8 * PAD], share) + grad_logit[None, :] * gate_share
    gate_total = jnp.sum(unit * (gain * w_gate)[:, None], axis=0)
    row_total = jnp.sum(back[8 * PAD : 8 * PAD + 3], axis=0) + grad_logit * gate_total
    unit_share = token_share * inverse
    scaled = total * gain_share
    grad_tokens = (
        grad_share + inverse * (scaled - unit_share * (row_total / model_width)[None, :])
    ).astype(BF16)
    return (layer_out.T, grad_tokens.T, steer_grad)


def solution(mesh):
    split = Mesh(mesh.devices.reshape(4, 8, 2, 4, 2), SEQ + HEAD)
    placed = (
        P(SEQ, None),
        P(),
        P(SEQ, HEAD),
        P(SEQ, HEAD),
        P(SEQ, HEAD),
        P(SEQ, HEAD),
        P(),
        P(),
        P(SEQ),
        P(SEQ),
        P(SEQ, None),
    )
    return jax.shard_map(
        shards,
        mesh=split,
        in_specs=placed,
        out_specs=(P(SEQ, HEAD), P(SEQ, HEAD), P(None, HEAD)),
        check_vma=False,
    )
```
